32 devices in a mesh: gossip: 16 (over z, y, core), group: 2 (over x).
Axes of the slice: x: 2, y: 2, z: 4, core: 2. Of those that a mesh axis runs over, the one named last changes fastest.
Arguments:
- weights: bfloat16 [32, 1024, 512], P(('gossip', 'group')), may hold values from -6 to 6
- inputs: bfloat16 [24576, 1024], P(('gossip', 'group')), may hold values from -6 to 6
- targets: bfloat16 [24576, 512], P(('gossip', 'group')), may hold values from -6 to 6
- peer_plan: int32 [3, 2], replicated, may hold values from 1 to 4
- shard_order: int32 [32, 3], P(('gossip', 'group')), may hold values from 0 to 2, each once within a row
Outputs:
- replica_weights: bfloat16 [32, 1024, 512], P(('gossip', 'group'))
- mean_weights: float32 [1024, 512], P(('gossip', 'group'))
The draws below stay inside these ranges and needn't reach their ends.
All inputs are finite; a program needn't handle non-finite values.
Results may differ from the reference program's by a relative error of at most 0.0054.
Values may be sent and summed in bfloat16 or wider, within the bound.
No kernel may reach another device: no remote copies, remote signals or barrier semaphores. Data moves between devices by JAX's collectives and lax.ppermute only.
A program may use at most 64 MiB of HBM per device.

```python
import math
import jax
import jax.numpy as jnp
from jax import lax

DIN = 1024
DOUT = 512
ROWS = 256
STEPS = 3
REPLICAS = 32
N_GOSSIP = 16
N_GROUP = 2


def plant(values, own_key, low, top_value):
    dims = values.shape
    spot = [jax.random.randint(jax.random.fold_in(own_key, axis), (), 0, dims[axis]) for axis in range(len(dims))]
    values = values.at[tuple(spot)].set(low)
    longest = dims.index(max(dims))
    spot[longest] = (spot[longest] + 1) % dims[longest]
    return values.at[tuple(spot)].set(top_value)


def strengthened(drawn, rng, source, target, shards_of, factor):
    owner, partner = [(jnp.arange(drawn.shape[position]) // (drawn.shape[position] // shards_of)).reshape([-1 if axis == position else 1 for axis in range(drawn.ndim)]) for position in (source, target)]
    chosen = jax.random.permutation(rng, shards_of)[partner]
    strong = (owner == chosen) | (owner == (partner + shards_of // 2) % shards_of)
    return jnp.where(strong, factor * drawn, drawn)


def steps_of(rng, extent, cuts, least, largest):
    def one(axis_at, parts):
        draws = jax.random.uniform(jax.random.fold_in(jax.random.fold_in(rng, 6), axis_at), (parts,), jnp.float32, least / len(cuts), largest / len(cuts))
        return jnp.repeat(jnp.exp(draws), extent[axis_at] // parts).reshape((-1,) + (1,) * (len(extent) - axis_at - 1))

    level = one(*cuts[0])
    for cut in cuts[1:]:
        level = level * one(*cut)
    return level


def normal_values(rng, shape, spread, reach, pieces=(), dtype=jnp.bfloat16):
    values = spread * jax.random.normal(rng, shape, jnp.float32)
    if pieces:
        values = values * steps_of(rng, shape, pieces, -0.22, 0.18)
    return jnp.clip(values, -reach, reach).astype(dtype)


def noise_with(stream_key, dims, width, bound, cuts, heavy, held_as=jnp.bfloat16):
    values = width * jax.random.normal(stream_key, dims, jnp.float32)
    if cuts:
        values = values * steps_of(stream_key, dims, cuts, -0.22, 0.18)
    return jnp.clip(strengthened(values, jax.random.fold_in(stream_key, 3), *heavy), -bound, bound).astype(held_as)


def setup_inputs(seed: int = 0) -> dict:
    keys = jax.random.split(jax.random.key(seed), 6)
    weights = noise_with(keys[0], (REPLICAS, DIN, DOUT), 1.0, 6.0, ((0, 32),), (0, 1, 32, 2.75))
    inputs = normal_values(keys[1], (REPLICAS * STEPS * ROWS, DIN), 1.0, 6.0, ((0, 32),))
    targets = normal_values(keys[2], (REPLICAS * STEPS * ROWS, DOUT), 1.0, 6.0, ((0, 32),))
    peer_plan = plant(jax.random.randint(keys[3], (STEPS, 2), 1, 5), jax.random.fold_in(keys[3], 1), 1, 4).astype(jnp.int32)
    shard_order = jax.vmap(lambda own: jax.random.permutation(own, STEPS))(jax.random.split(keys[4], REPLICAS)).reshape((REPLICAS, STEPS)).astype(jnp.int32)
    return {"weights": weights, "inputs": inputs, "targets": targets, "peer_plan": peer_plan, "shard_order": shard_order}


learning_rate = 0.3
momentum_decay = 0.9

def local_gradient(batch_in, batch_out, rounded):
    fan_scale = 1.0 / math.sqrt(batch_in.shape[1])
    preact = jnp.dot(batch_in, rounded, preferred_element_type=jnp.float32) * fan_scale
    normal_cdf = 0.5 * (1.0 + lax.erf(preact * (1.0 / math.sqrt(2.0))))
    normal_pdf = jnp.exp(-0.5 * preact * preact) * (1.0 / math.sqrt(2.0 * math.pi))
    residual = preact * normal_cdf - batch_out.astype(jnp.float32)
    derivative = normal_cdf + preact * normal_pdf
    delta = (residual * derivative).astype(jnp.bfloat16)
    product = lax.dot_general(batch_in, delta, (((0,), (0,)), ((), ())), preferred_element_type=jnp.float32)
    return product * fan_scale

def reference(weights, inputs, targets, peer_plan, shard_order):
    master = weights.astype(jnp.float32)
    velocity = jnp.zeros_like(master)
    input_blocks = inputs.reshape(REPLICAS, STEPS, ROWS, DIN)
    target_blocks = targets.reshape(REPLICAS, STEPS, ROWS, DOUT)
    for step_index in range(STEPS):
        rounded = master.astype(jnp.bfloat16)

        def one_replica(packed):
            own_weights, own_inputs, own_targets, shard_row = packed
            pick = shard_row[step_index].astype(jnp.int32)
            batch_in = lax.dynamic_index_in_dim(own_inputs, pick, 0, keepdims=False)
            batch_out = lax.dynamic_index_in_dim(own_targets, pick, 0, keepdims=False)
            return local_gradient(batch_in, batch_out, own_weights)
        gradients = lax.map(one_replica, (rounded, input_blocks, target_blocks, shard_order))
        velocity = momentum_decay * velocity + gradients
        neighbour = jnp.roll(rounded.reshape(N_GOSSIP, N_GROUP, DIN, DOUT), 2 ** step_index, axis=0)
        neighbour = neighbour.reshape(REPLICAS, DIN, DOUT).astype(jnp.float32)
        self_weight = peer_plan[step_index, 0].astype(jnp.float32)
        peer_weight = peer_plan[step_index, 1].astype(jnp.float32)
        master = (self_weight * master + peer_weight * neighbour) / (self_weight + peer_weight) - learning_rate * velocity
    replica_weights = master.astype(jnp.bfloat16)
    mean_weights = lax.optimization_barrier(jnp.sum(master, axis=0)) / REPLICAS
    return (replica_weights, mean_weights)
```

```python
import math

import jax
import jax.numpy as jnp
from jax import lax
from jax.sharding import PartitionSpec as P


STEPS = 3

learning_rate = 0.3
momentum_decay = 0.9


def shifted(value, axis, steps):
    count = lax.axis_size(axis)
    pairs = [(source, (source + steps) % count) for source in range(count)]
    return lax.ppermute(value, axis, pairs)


def flipped(value, axis, bit):
    count = lax.axis_size(axis)
    return lax.ppermute(value, axis, [(source, source ^ bit) for source in range(count)])


def local_gradient(batch_in, batch_out, rounded):
    fan_scale = 1.0 / math.sqrt(batch_in.shape[1])
    preact = jnp.dot(batch_in, rounded, preferred_element_type=jnp.float32) * fan_scale
    normal_cdf = 0.5 * (1.0 + lax.erf(preact * (1.0 / math.sqrt(2.0))))
    normal_pdf = jnp.exp(-0.5 * preact * preact) * (1.0 / math.sqrt(2.0 * math.pi))
    residual = preact * normal_cdf - batch_out.astype(jnp.float32)
    derivative = normal_cdf + preact * normal_pdf
    delta = (residual * derivative).astype(jnp.bfloat16)
    product = lax.dot_general(
        batch_in, delta, (((0,), (0,)), ((), ())), preferred_element_type=jnp.float32
    )
    return product * fan_scale


def scattered_sum(value):
    n_gossip, n_group = lax.axis_size("gossip"), lax.axis_size("group")
    gossip_bits, group_bits = n_gossip.bit_length() - 1, n_group.bit_length() - 1
    rows = value.shape[0]
    value = value.reshape((2,) * (gossip_bits + group_bits) + (rows // (n_gossip * n_group), value.shape[1]))
    left = [("gossip", bit) for bit in reversed(range(gossip_bits))]
    left += [("group", bit) for bit in reversed(range(group_bits))]
    order = [("gossip", 0)] + [("group", bit) for bit in range(group_bits)]
    order += [("gossip", bit) for bit in range(1, gossip_bits)]
    for axis, bit in order:
        place = left.index((axis, bit))
        mine = (lax.axis_index(axis) >> bit) & 1
        keep = lax.dynamic_index_in_dim(value, mine, place, keepdims=False)
        give = lax.dynamic_index_in_dim(value, 1 - mine, place, keepdims=False)
        arrived = flipped(give, axis, 1 << bit)
        value = keep + arrived
        left.pop(place)
    return value


def steps(weights, inputs, targets, peer_plan, shard_order):
    rounded = weights[0]
    master = rounded.astype(jnp.float32)
    velocity = None
    row_count = inputs.shape[0] // STEPS
    for step_index in range(STEPS):
        neighbour = shifted(rounded, "gossip", 2**step_index)
        shard_pick = shard_order[0, step_index]
        batch_in = lax.dynamic_slice_in_dim(inputs, shard_pick * row_count, row_count, 0)
        batch_out = lax.dynamic_slice_in_dim(targets, shard_pick * row_count, row_count, 0)
        gradient = local_gradient(batch_in, batch_out, rounded)
        velocity = gradient if velocity is None else momentum_decay * velocity + gradient
        plan = peer_plan[step_index].astype(jnp.float32)
        total = plan[0] + plan[1]
        own_share, peer_share = plan[0] / total, plan[1] / total
        base = lax.optimization_barrier(own_share * master - learning_rate * velocity)
        if step_index == STEPS - 1:
            part = lax.optimization_barrier(base + peer_share * rounded.astype(jnp.float32))
            replicas_all = lax.axis_size("gossip") * lax.axis_size("group")
            mean_weights = scattered_sum(part) / replicas_all
            mean_weights, neighbour = lax.optimization_barrier((mean_weights, neighbour))
        master = base + peer_share * neighbour.astype(jnp.float32)
        rounded = master.astype(jnp.bfloat16)
    return (rounded[None], mean_weights)


def solution(mesh):
    return jax.shard_map(
        steps,
        mesh=mesh,
        in_specs=(
            P(("gossip", "group"), None, None),
            P(("gossip", "group"), None),
            P(("gossip", "group"), None),
            P(),
            P(("gossip", "group"), None),
        ),
        out_specs=(P(("gossip", "group"), None, None), P(("gossip", "group"), None)),
        check_vma=False,
    )
```

```python
import functools
import math

import jax
import jax.numpy as jnp
from jax import lax
from jax.experimental import pallas as pl
from jax.experimental.pallas import tpu as pltpu
from jax.sharding import PartitionSpec as P


STEPS = 3
HALVES = 2
KERNEL_VMEM = 20 << 20

learning_rate = 0.3
momentum_decay = 0.9


def shifted(value, axis, steps):
    count = lax.axis_size(axis)
    pairs = [(source, (source + steps) % count) for source in range(count)]
    return lax.ppermute(value, axis, pairs)


def flipped(value, axis, bit):
    count = lax.axis_size(axis)
    return lax.ppermute(value, axis, [(source, source ^ bit) for source in range(count)])


def shares(plan_ref, step):
    own = plan_ref[step, 0].astype(jnp.float32)
    peer = plan_ref[step, 1].astype(jnp.float32)
    own, peer = jnp.full((1, 1), own), jnp.full((1, 1), peer)
    return own / (own + peer), peer / (own + peer)


def gradient_of(batch_in, batch_out, rounded):
    fan_scale = 1.0 / math.sqrt(batch_in.shape[1])
    preact = jnp.dot(batch_in, rounded, preferred_element_type=jnp.float32) * fan_scale
    normal_cdf = 0.5 * (1.0 + lax.erf(preact * (1.0 / math.sqrt(2.0))))
    normal_pdf = jnp.exp(-0.5 * preact * preact) * (1.0 / math.sqrt(2.0 * math.pi))
    residual = preact * normal_cdf - batch_out.astype(jnp.float32)
    derivative = normal_cdf + preact * normal_pdf
    delta = (residual * derivative).astype(jnp.bfloat16)
    product = lax.dot_general(
        batch_in, delta, (((0,), (0,)), ((), ())), preferred_element_type=jnp.float32
    )
    return product * fan_scale


def shard_of(order, x, t, step, columns):
    batch = x.shape[0] // STEPS
    rows = pl.ds(pl.multiple_of(order[0, step] * batch, batch), batch)
    return x[rows, :], t[rows, columns]


def first_kernel(order, plan, x, t, w, base, velocity):
    own, _ = shares(plan, 0)
    width = w.shape[1] // HALVES
    for half in range(HALVES):
        columns = slice(half * width, (half + 1) * width)
        gradient = gradient_of(*shard_of(order, x, t, 0, columns), w[:, columns])
        velocity[:, columns] = gradient
        base[:, columns] = own * w[:, columns].astype(jnp.float32) - learning_rate * gradient


def middle_kernel(columns, order, plan, x, t, rounded, base_in, arrived, velocity_in, base, velocity):
    _, peer = shares(plan, 0)
    own, _ = shares(plan, 1)
    v = momentum_decay * velocity_in[:, columns] + gradient_of(*shard_of(order, x, t, 1, columns), rounded[...])
    velocity[...] = v
    master = base_in[:, columns] + peer * arrived[:, columns].astype(jnp.float32)
    base[...] = own * master - learning_rate * v


def last_kernel(columns, split, order, plan, x, t, rounded, base_in, arrived, velocity_in, base, *outs):
    _, peer = shares(plan, STEPS - 2)
    own, last_peer = shares(plan, STEPS - 1)
    r = rounded[...]
    v = momentum_decay * velocity_in[...] + gradient_of(*shard_of(order, x, t, STEPS - 1, columns), r)
    master = base_in[...] + peer * arrived[...].astype(jnp.float32)
    b = own * master - learning_rate * v
    base[...] = b
    part = b + last_peer * r.astype(jnp.float32)
    if not split:
        outs[0][...] = part
        return
    keep, give, held = outs
    held[...] = part.reshape(held.shape)
    mine = lax.axis_index("gossip") & 1
    keep[...] = held[:, pl.ds(mine, 1)].reshape(keep.shape)
    give[...] = held[:, pl.ds(1 - mine, 1)].reshape(give.shape)


def round_kernel(step, plan, base, arrived, *rounded):
    _, peer = shares(plan, step)
    width = base.shape[1] // len(rounded)
    for i, r in enumerate(rounded):
        columns = slice(i * width, (i + 1) * width)
        r[...] = (base[:, columns] + peer * arrived[:, columns].astype(jnp.float32)).astype(jnp.bfloat16)


def finish_kernel(plan, *refs):
    _, peer = shares(plan, STEPS - 1)
    out = refs[-1]
    width = out.shape[1] // HALVES
    for i in range(HALVES):
        base, arrived = refs[2 * i], refs[2 * i + 1]
        out[:, i * width:(i + 1) * width] = (base[...] + peer * arrived[...].astype(jnp.float32)).astype(jnp.bfloat16)


def leg_kernel(axis, bit, *refs):
    keep, give = refs[-2:]
    pairs = refs[:-2]
    width = 2 * keep.shape[-1] // len(pairs)
    mine = (lax.axis_index(axis) >> bit) & 1
    for i in range(len(pairs) // 2):
        kept, arrived = pairs[2 * i], pairs[2 * i + 1]
        columns = slice(i * width, (i + 1) * width)
        for out, side in ((keep, mine), (give, 1 - mine)):
            at = pl.ds(side, 1)
            total = kept[:, at] + arrived[:, at].astype(jnp.float32)
            out[:, :, columns] = total.reshape(out.shape[:-1] + (width,)).astype(out.dtype)


def spread_kernel(kept, arrived, keep, *gives):
    mine = lax.axis_index("gossip") >> 2
    for other, out in enumerate((keep,) + gives):
        at = pl.ds(mine ^ other, 1)
        total = kept[at] + arrived[at].astype(jnp.float32)
        out[...] = total.reshape(out.shape).astype(out.dtype)


def mean_kernel(replicas, keep, *refs):
    total = keep[...]
    for arrived in refs[:-1]:
        total = total + arrived[...].astype(jnp.float32)
    refs[-1][...] = total / replicas


def call(kernel, ins, outs, scratch=()):
    in_vmem, in_smem = pl.BlockSpec(memory_space=pltpu.VMEM), pl.BlockSpec(memory_space=pltpu.SMEM)
    return pl.pallas_call(
        kernel,
        in_specs=[in_smem if array.dtype == jnp.int32 else in_vmem for array in ins],
        out_specs=[in_vmem] * len(outs),
        out_shape=[jax.ShapeDtypeStruct(shape, dtype) for shape, dtype in outs],
        scratch_shapes=list(scratch),
        compiler_params=pltpu.CompilerParams(vmem_limit_bytes=KERNEL_VMEM),
    )(*ins)


def scattered_sum(value):
    n_gossip, n_group = lax.axis_size("gossip"), lax.axis_size("group")
    gossip_bits, group_bits = n_gossip.bit_length() - 1, n_group.bit_length() - 1
    rows = value.shape[0]
    value = value.reshape((2,) * (gossip_bits + group_bits) + (rows // (n_gossip * n_group), value.shape[1]))
    left = [("gossip", bit) for bit in reversed(range(gossip_bits))]
    left += [("group", bit) for bit in reversed(range(group_bits))]
    order = [("gossip", 0)] + [("group", bit) for bit in range(group_bits)]
    order += [("gossip", bit) for bit in range(1, gossip_bits)]
    for axis, bit in order:
        place = left.index((axis, bit))
        mine = (lax.axis_index(axis) >> bit) & 1
        keep = lax.dynamic_index_in_dim(value, mine, place, keepdims=False)
        give = lax.dynamic_index_in_dim(value, 1 - mine, place, keepdims=False)
        value = keep + flipped(give, axis, 1 << bit)
        left.pop(place)
    return value


def leg(pairs, axis, bit):
    lead, _, rows, width = pairs[0][0].shape
    shape = (lead, rows, width * len(pairs))
    ins = [array for pair in pairs for array in pair]
    return call(functools.partial(leg_kernel, axis, bit), ins, [(shape, jnp.float32), (shape, jnp.bfloat16)])


def steps(weights, inputs, targets, plan, order):
    n_gossip, n_group = lax.axis_size("gossip"), lax.axis_size("group")
    replicas = n_gossip * n_group
    weights = weights[0]
    din, dout = weights.shape
    width = dout // HALVES
    own_rows = din // replicas
    split = own_rows % 16 == 0 and n_group == 2 and n_gossip % 4 == 0
    columns = [slice(half * width, (half + 1) * width) for half in range(HALVES)]
    half_f32, half_bf16 = ((din, width), jnp.float32), ((din, width), jnp.bfloat16)

    arrived0 = shifted(weights, "gossip", 1)
    base0, velocity0 = call(
        first_kernel, [order, plan, inputs, targets, weights], [((din, dout), jnp.float32)] * 2
    )
    rounded1 = call(functools.partial(round_kernel, 0), [plan, base0, arrived0], [half_bf16] * HALVES)
    arrived1, middles = [], []
    for half in range(HALVES):
        arrived1.append(shifted(rounded1[half], "gossip", 2))
    for half in range(HALVES):
        middles.append(
            call(
                functools.partial(middle_kernel, columns[half]),
                [order, plan, inputs, targets, rounded1[half], base0, arrived0, velocity0],
                [half_f32] * 2,
            )
        )
    parts, last = [], []
    for half in range(HALVES):
        base1, velocity1 = middles[half]
        (rounded2,) = call(functools.partial(round_kernel, 1), [plan, base1, arrived1[half]], [half_bf16])
        arrived2 = shifted(rounded2, "gossip", 4)
        outs, scratch = [half_f32] * 2, ()
        if split:
            pair = (n_gossip // 2, n_group * own_rows, width)
            outs = [half_f32, (pair, jnp.float32), (pair, jnp.float32)]
            scratch = (pltpu.VMEM((pair[0], 2) + pair[1:], jnp.float32),)
        base2, *part = call(
            functools.partial(last_kernel, columns[half], split),
            [order, plan, inputs, targets, rounded2, base1, arrived1[half], velocity1],
            outs,
            scratch,
        )
        last += [base2, arrived2]
        if not split:
            parts.append(part[0])
            continue
        keep, give = part
        got = flipped(give, "gossip", 1)
        view = (n_gossip // 2, n_group, own_rows, width)
        keep, give = leg([(keep.reshape(view), got.reshape(view))], "group", 0)
        got = flipped(give, "group", 1)
        parts.append((keep, got))
    if split:
        view = (n_gossip // 4, 2, own_rows, width)
        keep, give = leg([(keep.reshape(view), got.reshape(view)) for keep, got in parts], "gossip", 1)
        got = flipped(give, "gossip", 2)
        shape = (own_rows, dout)
        others = [(shape, jnp.bfloat16)] * (n_gossip // 4 - 1)
        keep, *gives = call(spread_kernel, [keep, got], [(shape, jnp.float32)] + others)
        gots = []
        for other, give in enumerate(gives, 1):
            gots.append(flipped(give, "gossip", 4 * other))
        (mean_weights,) = call(functools.partial(mean_kernel, replicas), [keep] + gots, [(shape, jnp.float32)])
    else:
        mean_weights = scattered_sum(jnp.concatenate(parts, axis=1)) / replicas
    (replica_weights,) = call(finish_kernel, [plan] + last, [((din, dout), jnp.bfloat16)])
    return (replica_weights[None], mean_weights)


def solution(mesh):
    return jax.shard_map(
        steps,
        mesh=mesh,
        in_specs=(
            P(("gossip", "group"), None, None),
            P(("gossip", "group"), None),
            P(("gossip", "group"), None),
            P(),
            P(("gossip", "group"), None),
        ),
        out_specs=(P(("gossip", "group"), None, None), P(("gossip", "group"), None)),
        check_vma=False,
    )
```

```python
import functools
import math

import jax
import jax.numpy as jnp
from jax import lax
from jax.experimental import pallas as pl
from jax.experimental.pallas import tpu as pltpu
from jax.sharding import PartitionSpec as P


STEPS = 3
HALVES = 2
KERNEL_VMEM = 20 << 20

learning_rate = 0.3
momentum_decay = 0.9


def shifted(value, axis, steps):
    count = lax.axis_size(axis)
    pairs = [(source, (source + steps) % count) for source in range(count)]
    return lax.ppermute(value, axis, pairs)


def flipped(value, axis, bit):
    count = lax.axis_size(axis)
    return lax.ppermute(value, axis, [(source, source ^ bit) for source in range(count)])


def shares(plan_ref, step):
    own = plan_ref[step, 0].astype(jnp.float32)
    peer = plan_ref[step, 1].astype(jnp.float32)
    own, peer = jnp.full((1, 1), own), jnp.full((1, 1), peer)
    return own / (own + peer), peer / (own + peer)


def gradient_of(batch_in, batch_out, rounded):
    fan_scale = 1.0 / math.sqrt(batch_in.shape[1])
    preact = jnp.dot(batch_in, rounded, preferred_element_type=jnp.float32) * fan_scale
    normal_cdf = 0.5 * (1.0 + lax.erf(preact * (1.0 / math.sqrt(2.0))))
    normal_pdf = jnp.exp(-0.5 * preact * preact) * (1.0 / math.sqrt(2.0 * math.pi))
    residual = preact * normal_cdf - batch_out.astype(jnp.float32)
    derivative = normal_cdf + preact * normal_pdf
    delta = (residual * derivative).astype(jnp.bfloat16)
    product = lax.dot_general(
        batch_in, delta, (((0,), (0,)), ((), ())), preferred_element_type=jnp.float32
    )
    return product * fan_scale


def shard_of(order, x, t, step, columns):
    batch = x.shape[0] // STEPS
    rows = pl.ds(pl.multiple_of(order[0, step] * batch, batch), batch)
    return x[rows, :], t[rows, columns]


def first_kernel(order, plan, x, t, w, base, velocity):
    own, _ = shares(plan, 0)
    width = w.shape[1] // HALVES
    for half in range(HALVES):
        columns = slice(half * width, (half + 1) * width)
        gradient = gradient_of(*shard_of(order, x, t, 0, columns), w[:, columns])
        velocity[:, columns] = gradient
        base[:, columns] = own * w[:, columns].astype(jnp.float32) - learning_rate * gradient


def middle_kernel(columns, order, plan, x, t, rounded, base_in, arrived, velocity_in, base, velocity):
    _, peer = shares(plan, 0)
    own, _ = shares(plan, 1)
    v = momentum_decay * velocity_in[:, columns] + gradient_of(*shard_of(order, x, t, 1, columns), rounded[...])
    velocity[...] = v
    master = base_in[:, columns] + peer * arrived[:, columns].astype(jnp.float32)
    base[...] = own * master - learning_rate * v


def last_kernel(columns, split, order, plan, x, t, rounded, base_in, arrived, velocity_in, base, *outs):
    _, peer = shares(plan, STEPS - 2)
    own, last_peer = shares(plan, STEPS - 1)
    r = rounded[...]
    v = momentum_decay * velocity_in[...] + gradient_of(*shard_of(order, x, t, STEPS - 1, columns), r)
    master = base_in[...] + peer * arrived[...].astype(jnp.float32)
    b = own * master - learning_rate * v
    base[...] = b
    part = b + last_peer * r.astype(jnp.float32)
    if not split:
        outs[0][...] = part
        return
    keep, give, held = outs
    held[...] = part.reshape(held.shape)
    mine = lax.axis_index("gossip") & 1
    keep[...] = held[:, pl.ds(mine, 1)].reshape(keep.shape)
    give[...] = held[:, pl.ds(1 - mine, 1)].reshape(give.shape)


def round_kernel(step, plan, base, arrived, *rounded):
    _, peer = shares(plan, step)
    width = base.shape[1] // len(rounded)
    for i, r in enumerate(rounded):
        columns = slice(i * width, (i + 1) * width)
        r[...] = (base[:, columns] + peer * arrived[:, columns].astype(jnp.float32)).astype(jnp.bfloat16)


def finish_kernel(plan, *refs):
    _, peer = shares(plan, STEPS - 1)
    out = refs[-1]
    width = out.shape[1] // HALVES
    for i in range(HALVES):
        base, arrived = refs[2 * i], refs[2 * i + 1]
        out[:, i * width:(i + 1) * width] = (base[...] + peer * arrived[...].astype(jnp.float32)).astype(jnp.bfloat16)


def leg_kernel(axis, bit, kept, arrived, keep, give):
    mine = (lax.axis_index(axis) >> bit) & 1
    for out, side in ((keep, mine), (give, 1 - mine)):
        at = pl.ds(side, 1)
        total = kept[:, at] + arrived[:, at].astype(jnp.float32)
        out[...] = total.reshape(out.shape).astype(out.dtype)


def corner_kernel(first, first_arrived, second, second_arrived, keep, give_y, give_x, give_xy):
    y, x = (lax.axis_index("gossip") >> 1) & 1, lax.axis_index("group") & 1
    width = first.shape[-1]
    for out, row in ((keep, y), (give_y, 1 - y)):
        at, column = pl.ds(row, 1), pl.ds(x, 1)
        total = first[:, at] + first_arrived[:, at].astype(jnp.float32)
        out[:, :, :width] = total.reshape(out.shape[:-1] + (width,)).astype(out.dtype)
        total = second[:, at, column] + second_arrived[:, at, column]
        out[:, :, width:] = total.reshape(out.shape[:-1] + (width,)).astype(out.dtype)
    for out, row in ((give_x, y), (give_xy, 1 - y)):
        at, column = pl.ds(row, 1), pl.ds(1 - x, 1)
        total = second[:, at, column] + second_arrived[:, at, column]
        out[...] = total.reshape(out.shape).astype(out.dtype)


def spread_kernel(kept, from_y, from_x, from_xy, keep, *gives):
    mine = lax.axis_index("gossip") >> 2
    width = from_x.shape[-1]
    for other, out in enumerate((keep,) + gives):
        at = pl.ds(mine ^ other, 1)
        rows = kept[at] + from_y[at].astype(jnp.float32)
        late = from_x[at].astype(jnp.float32) + from_xy[at].astype(jnp.float32)
        out[:, :width] = rows[:, :, :width].reshape(out.shape[0], width).astype(out.dtype)
        out[:, width:] = (rows[:, :, width:] + late).reshape(out.shape[0], width).astype(out.dtype)


def mean_kernel(replicas, keep, *refs):
    total = keep[...]
    for arrived in refs[:-1]:
        total = total + arrived[...].astype(jnp.float32)
    refs[-1][...] = total / replicas


def call(kernel, ins, outs, scratch=()):
    in_vmem, in_smem = pl.BlockSpec(memory_space=pltpu.VMEM), pl.BlockSpec(memory_space=pltpu.SMEM)
    return pl.pallas_call(
        kernel,
        in_specs=[in_smem if array.dtype == jnp.int32 else in_vmem for array in ins],
        out_specs=[in_vmem] * len(outs),
        out_shape=[jax.ShapeDtypeStruct(shape, dtype) for shape, dtype in outs],
        scratch_shapes=list(scratch),
        compiler_params=pltpu.CompilerParams(vmem_limit_bytes=KERNEL_VMEM),
    )(*ins)


def scattered_sum(value):
    n_gossip, n_group = lax.axis_size("gossip"), lax.axis_size("group")
    gossip_bits, group_bits = n_gossip.bit_length() - 1, n_group.bit_length() - 1
    rows = value.shape[0]
    value = value.reshape((2,) * (gossip_bits + group_bits) + (rows // (n_gossip * n_group), value.shape[1]))
    left = [("gossip", bit) for bit in reversed(range(gossip_bits))]
    left += [("group", bit) for bit in reversed(range(group_bits))]
    order = [("gossip", 0)] + [("group", bit) for bit in range(group_bits)]
    order += [("gossip", bit) for bit in range(1, gossip_bits)]
    for axis, bit in order:
        place = left.index((axis, bit))
        mine = (lax.axis_index(axis) >> bit) & 1
        keep = lax.dynamic_index_in_dim(value, mine, place, keepdims=False)
        give = lax.dynamic_index_in_dim(value, 1 - mine, place, keepdims=False)
        value = keep + flipped(give, axis, 1 << bit)
        left.pop(place)
    return value


def steps(weights, inputs, targets, plan, order):
    n_gossip, n_group = lax.axis_size("gossip"), lax.axis_size("group")
    replicas = n_gossip * n_group
    weights = weights[0]
    din, dout = weights.shape
    width = dout // HALVES
    own_rows = din // replicas
    split = own_rows % 16 == 0 and n_group == 2 and n_gossip % 4 == 0
    columns = [slice(half * width, (half + 1) * width) for half in range(HALVES)]
    half_f32, half_bf16 = ((din, width), jnp.float32), ((din, width), jnp.bfloat16)

    arrived0 = shifted(weights, "gossip", 1)
    base0, velocity0 = call(
        first_kernel, [order, plan, inputs, targets, weights], [((din, dout), jnp.float32)] * 2
    )
    rounded1 = call(functools.partial(round_kernel, 0), [plan, base0, arrived0], [half_bf16] * HALVES)
    arrived1, middles = [], []
    for half in range(HALVES):
        arrived1.append(shifted(rounded1[half], "gossip", 2))
    for half in range(HALVES):
        middles.append(
            call(
                functools.partial(middle_kernel, columns[half]),
                [order, plan, inputs, targets, rounded1[half], base0, arrived0, velocity0],
                [half_f32] * 2,
            )
        )
    parts, last = [], []
    for half in range(HALVES):
        base1, velocity1 = middles[half]
        (rounded2,) = call(functools.partial(round_kernel, 1), [plan, base1, arrived1[half]], [half_bf16])
        arrived2 = shifted(rounded2, "gossip", 4)
        outs, scratch = [half_f32] * 2, ()
        if split:
            pair = (n_gossip // 2, n_group * own_rows, width)
            outs = [half_f32, (pair, jnp.float32), (pair, jnp.float32)]
            scratch = (pltpu.VMEM((pair[0], 2) + pair[1:], jnp.float32),)
        base2, *part = call(
            functools.partial(last_kernel, columns[half], split),
            [order, plan, inputs, targets, rounded2, base1, arrived1[half], velocity1],
            outs,
            scratch,
        )
        last += [base2, arrived2]
        if not split:
            parts.append(part[0])
            continue
        keep, give = part
        got = flipped(give, "gossip", 1)
        if half < HALVES - 1:
            view = (n_gossip // 2, n_group, own_rows, width)
            shape = (n_gossip // 2, own_rows, width)
            keep, give = call(
                functools.partial(leg_kernel, "group", 0),
                [keep.reshape(view), got.reshape(view)],
                [(shape, jnp.float32), (shape, jnp.bfloat16)],
            )
            got = flipped(give, "group", 1)
        parts += [keep, got]
    if split:
        lead = n_gossip // 4
        view = (lead, 2, own_rows, width)
        deep = (lead, 2, n_group, own_rows, width)
        wide, narrow = (lead, own_rows, dout), (lead, own_rows, width)
        keep, give_y, give_x, give_xy = call(
            corner_kernel,
            [parts[0].reshape(view), parts[1].reshape(view), parts[2].reshape(deep), parts[3].reshape(deep)],
            [(wide, jnp.float32), (wide, jnp.bfloat16), (narrow, jnp.bfloat16), (narrow, jnp.bfloat16)],
        )
        from_x = flipped(give_x, "group", 1)
        from_y = flipped(give_y, "gossip", 2)
        pairs = [(source, source ^ (2 * n_group + 1)) for source in range(replicas)]
        from_xy = lax.ppermute(give_xy, ("gossip", "group"), pairs)
        shape = (own_rows, dout)
        others = [(shape, jnp.bfloat16)] * (lead - 1)
        keep, *gives = call(spread_kernel, [keep, from_y, from_x, from_xy], [(shape, jnp.float32)] + others)
        gots = []
        for other, give in enumerate(gives, 1):
            gots.append(flipped(give, "gossip", 4 * other))
        (mean_weights,) = call(functools.partial(mean_kernel, replicas), [keep] + gots, [(shape, jnp.float32)])
    else:
        mean_weights = scattered_sum(jnp.concatenate(parts, axis=1)) / replicas
    (replica_weights,) = call(finish_kernel, [plan] + last, [((din, dout), jnp.bfloat16)])
    return (replica_weights[None], mean_weights)


def solution(mesh):
    return jax.shard_map(
        steps,
        mesh=mesh,
        in_specs=(
            P(("gossip", "group"), None, None),
            P(("gossip", "group"), None),
            P(("gossip", "group"), None),
            P(),
            P(("gossip", "group"), None),
        ),
        out_specs=(P(("gossip", "group"), None, None), P(("gossip", "group"), None)),
        check_vma=False,
    )
```

```python
import functools
import math

import jax
import jax.numpy as jnp
from jax import lax
from jax.experimental import pallas as pl
from jax.experimental.pallas import tpu as pltpu
from jax.sharding import PartitionSpec as P


STEPS = 3
HALVES = 2
KERNEL_VMEM = 20 << 20

learning_rate = 0.3
momentum_decay = 0.9


def shifted(value, axis, steps):
    count = lax.axis_size(axis)
    pairs = [(source, (source + steps) % count) for source in range(count)]
    return lax.ppermute(value, axis, pairs)


def moved(value, target):
    count = lax.axis_size("gossip")
    pairs = [(source, target(source) % count) for source in range(count) if target(source) is not None]
    return lax.ppermute(value, "gossip", pairs)


def flipped(value, axis, bit):
    count = lax.axis_size(axis)
    return lax.ppermute(value, axis, [(source, source ^ bit) for source in range(count)])


def shares(plan_ref, step):
    own = plan_ref[step, 0].astype(jnp.float32)
    peer = plan_ref[step, 1].astype(jnp.float32)
    own, peer = jnp.full((1, 1), own), jnp.full((1, 1), peer)
    return own / (own + peer), peer / (own + peer)


def gradient_of(batch_in, batch_out, rounded):
    fan_scale = 1.0 / math.sqrt(batch_in.shape[1])
    preact = jnp.dot(batch_in, rounded, preferred_element_type=jnp.float32) * fan_scale
    normal_cdf = 0.5 * (1.0 + lax.erf(preact * (1.0 / math.sqrt(2.0))))
    normal_pdf = jnp.exp(-0.5 * preact * preact) * (1.0 / math.sqrt(2.0 * math.pi))
    residual = preact * normal_cdf - batch_out.astype(jnp.float32)
    derivative = normal_cdf + preact * normal_pdf
    delta = (residual * derivative).astype(jnp.bfloat16)
    product = lax.dot_general(
        batch_in, delta, (((0,), (0,)), ((), ())), preferred_element_type=jnp.float32
    )
    return product * fan_scale


def shard_of(order, x, t, step, columns):
    batch = x.shape[0] // STEPS
    rows = pl.ds(pl.multiple_of(order[0, step] * batch, batch), batch)
    return x[rows, :], t[rows, columns]


def first_kernel(order, plan, x, t, w, base, velocity):
    own, _ = shares(plan, 0)
    width = w.shape[1] // HALVES
    for half in range(HALVES):
        columns = slice(half * width, (half + 1) * width)
        gradient = gradient_of(*shard_of(order, x, t, 0, columns), w[:, columns])
        velocity[:, columns] = gradient
        base[:, columns] = own * w[:, columns].astype(jnp.float32) - learning_rate * gradient


def middle_kernel(columns, order, plan, x, t, rounded, master, velocity_in, base, velocity):
    own, _ = shares(plan, 1)
    v = momentum_decay * velocity_in[:, columns] + gradient_of(*shard_of(order, x, t, 1, columns), rounded[...])
    velocity[...] = v
    base[...] = own * master[...] - learning_rate * v


def last_kernel(columns, split, order, plan, x, t, rounded, master, velocity_in, base, *outs):
    own, last_peer = shares(plan, STEPS - 1)
    r = rounded[...]
    v = momentum_decay * velocity_in[...] + gradient_of(*shard_of(order, x, t, STEPS - 1, columns), r)
    b = own * master[...] - learning_rate * v
    base[...] = b
    part = b + last_peer * r.astype(jnp.float32)
    if not split:
        outs[0][...] = part
        return
    keep, give, held = outs
    held[...] = part.reshape(held.shape)
    mine = lax.axis_index("gossip") & 1
    keep[...] = held[:, pl.ds(mine, 1)].reshape(keep.shape)
    give[...] = held[:, pl.ds(1 - mine, 1)].reshape(give.shape)


def early_kernel(plan, base, arrived, *rounded):
    _, peer = shares(plan, 0)
    width = base.shape[1] // len(rounded)
    for i, r in enumerate(rounded):
        columns = slice(i * width, (i + 1) * width)
        r[...] = (base[:, columns] + peer * arrived[:, columns].astype(jnp.float32)).astype(jnp.bfloat16)


def round_kernel(step, halves, plan, base, *refs):
    _, peer = shares(plan, step)
    at = lax.axis_index("gossip")
    core, chip = at & 1, (at >> 1) & 1
    arrays, outs = refs[:-2 * halves], refs[-2 * halves:]
    width = base.shape[1] // halves
    for i in range(halves):
        columns = slice(i * width, (i + 1) * width)
        direct, *others = [array[:, columns].astype(jnp.float32) for array in arrays]
        arrived = direct
        if len(others) == 1:
            arrived = jnp.where(core == 1, others[0], direct)
        elif others:
            arrived = jnp.where(core == 1, jnp.where(chip == 1, others[0], others[1]), direct)
        master = base[:, columns] + peer * arrived
        outs[2 * i][...] = master.astype(jnp.bfloat16)
        outs[2 * i + 1][...] = master


def finish_kernel(plan, *refs):
    _, peer = shares(plan, STEPS - 1)
    out = refs[-1]
    width = out.shape[1] // HALVES
    for i in range(HALVES):
        base, arrived = refs[2 * i], refs[2 * i + 1]
        out[:, i * width:(i + 1) * width] = (base[...] + peer * arrived[...].astype(jnp.float32)).astype(jnp.bfloat16)


def leg_kernel(axis, bit, kept, arrived, keep, give):
    mine = (lax.axis_index(axis) >> bit) & 1
    for out, side in ((keep, mine), (give, 1 - mine)):
        at = pl.ds(side, 1)
        total = kept[:, at] + arrived[:, at].astype(jnp.float32)
        out[...] = total.reshape(out.shape).astype(out.dtype)


def corner_kernel(first, first_arrived, second, second_arrived, keep, give_y, give_x, give_xy):
    y, x = (lax.axis_index("gossip") >> 1) & 1, lax.axis_index("group") & 1
    width = first.shape[-1]
    for out, row in ((keep, y), (give_y, 1 - y)):
        at, column = pl.ds(row, 1), pl.ds(x, 1)
        total = first[:, at] + first_arrived[:, at].astype(jnp.float32)
        out[:, :, :width] = total.reshape(out.shape[:-1] + (width,)).astype(out.dtype)
        total = second[:, at, column] + second_arrived[:, at, column]
        out[:, :, width:] = total.reshape(out.shape[:-1] + (width,)).astype(out.dtype)
    for out, row in ((give_x, y), (give_xy, 1 - y)):
        at, column = pl.ds(row, 1), pl.ds(1 - x, 1)
        total = second[:, at, column] + second_arrived[:, at, column]
        out[...] = total.reshape(out.shape).astype(out.dtype)


def spread_kernel(kept, from_y, from_x, from_xy, keep, *gives):
    mine = lax.axis_index("gossip") >> 2
    width = from_x.shape[-1]
    for other, out in enumerate((keep,) + gives):
        at = pl.ds(mine ^ other, 1)
        rows = kept[at] + from_y[at].astype(jnp.float32)
        late = from_x[at].astype(jnp.float32) + from_xy[at].astype(jnp.float32)
        out[:, :width] = rows[:, :, :width].reshape(out.shape[0], width).astype(out.dtype)
        out[:, width:] = (rows[:, :, width:] + late).reshape(out.shape[0], width).astype(out.dtype)


def mean_kernel(replicas, keep, *refs):
    total = keep[...]
    for arrived in refs[:-1]:
        total = total + arrived[...].astype(jnp.float32)
    refs[-1][...] = total / replicas


def call(kernel, ins, outs, scratch=()):
    in_vmem, in_smem = pl.BlockSpec(memory_space=pltpu.VMEM), pl.BlockSpec(memory_space=pltpu.SMEM)
    return pl.pallas_call(
        kernel,
        in_specs=[in_smem if array.dtype == jnp.int32 else in_vmem for array in ins],
        out_specs=[in_vmem] * len(outs),
        out_shape=[jax.ShapeDtypeStruct(shape, dtype) for shape, dtype in outs],
        scratch_shapes=list(scratch),
        compiler_params=pltpu.CompilerParams(vmem_limit_bytes=KERNEL_VMEM),
    )(*ins)


def scattered_sum(value):
    n_gossip, n_group = lax.axis_size("gossip"), lax.axis_size("group")
    gossip_bits, group_bits = n_gossip.bit_length() - 1, n_group.bit_length() - 1
    rows = value.shape[0]
    value = value.reshape((2,) * (gossip_bits + group_bits) + (rows // (n_gossip * n_group), value.shape[1]))
    left = [("gossip", bit) for bit in reversed(range(gossip_bits))]
    left += [("group", bit) for bit in reversed(range(group_bits))]
    order = [("gossip", 0)] + [("group", bit) for bit in range(group_bits)]
    order += [("gossip", bit) for bit in range(1, gossip_bits)]
    for axis, bit in order:
        place = left.index((axis, bit))
        mine = (lax.axis_index(axis) >> bit) & 1
        keep = lax.dynamic_index_in_dim(value, mine, place, keepdims=False)
        give = lax.dynamic_index_in_dim(value, 1 - mine, place, keepdims=False)
        value = keep + flipped(give, axis, 1 << bit)
        left.pop(place)
    return value


def steps(weights, inputs, targets, plan, order):
    n_gossip, n_group = lax.axis_size("gossip"), lax.axis_size("group")
    replicas = n_gossip * n_group
    weights = weights[0]
    din, dout = weights.shape
    width = dout // HALVES
    own_rows = din // replicas
    split = own_rows % 16 == 0 and n_group == 2 and n_gossip % 4 == 0
    columns = [slice(half * width, (half + 1) * width) for half in range(HALVES)]
    half_f32, half_bf16 = ((din, width), jnp.float32), ((din, width), jnp.bfloat16)

    ship = moved(weights, lambda at: at + 1 if at & 1 else None)
    chip = moved(weights, lambda at: None if at & 1 else at + 1)
    base0, velocity0 = call(
        first_kernel, [order, plan, inputs, targets, weights], [((din, dout), jnp.float32)] * 2
    )
    early = call(early_kernel, [plan, base0, chip], [half_bf16] * HALVES)
    hops, sends, relays = [], [], []
    for half in range(HALVES):
        hops.append(moved(early[half], lambda at: at ^ 2 if at & 1 else None))
    firsts = call(functools.partial(round_kernel, 0, HALVES), [plan, base0, ship, chip], [half_bf16, half_f32] * HALVES)
    for half in range(HALVES):
        sends.append(moved(firsts[2 * half], lambda at: None if at & 1 else at + 2))
    middles = []
    for half in range(HALVES):
        middles.append(
            call(
                functools.partial(middle_kernel, columns[half]),
                [order, plan, inputs, targets] + list(firsts[2 * half:2 * half + 2]) + [velocity0],
                [half_f32] * 2,
            )
        )
    for half in range(HALVES):
        relays.append(moved(hops[half], lambda at: at + 4 if at & 3 == 1 else None))
    parts, last = [], []
    for half in range(HALVES):
        base1, velocity1 = middles[half]
        rounded2, master2 = call(
            functools.partial(round_kernel, 1, 1),
            [plan, base1, sends[half], hops[half], relays[half]],
            [half_bf16, half_f32],
        )
        arrived2 = shifted(rounded2, "gossip", 4)
        outs, scratch = [half_f32] * 2, ()
        if split:
            pair = (n_gossip // 2, n_group * own_rows, width)
            outs = [half_f32, (pair, jnp.float32), (pair, jnp.float32)]
            scratch = (pltpu.VMEM((pair[0], 2) + pair[1:], jnp.float32),)
        base2, *part = call(
            functools.partial(last_kernel, columns[half], split),
            [order, plan, inputs, targets, rounded2, master2, velocity1],
            outs,
            scratch,
        )
        last += [base2, arrived2]
        if not split:
            parts.append(part[0])
            continue
        keep, give = part
        got = flipped(give, "gossip", 1)
        if half < HALVES - 1:
            view = (n_gossip // 2, n_group, own_rows, width)
            shape = (n_gossip // 2, own_rows, width)
            keep, give = call(
                functools.partial(leg_kernel, "group", 0),
                [keep.reshape(view), got.reshape(view)],
                [(shape, jnp.float32), (shape, jnp.bfloat16)],
            )
            got = flipped(give, "group", 1)
        parts += [keep, got]
    if split:
        lead = n_gossip // 4
        view = (lead, 2, own_rows, width)
        deep = (lead, 2, n_group, own_rows, width)
        wide, narrow = (lead, own_rows, dout), (lead, own_rows, width)
        keep, give_y, give_x, give_xy = call(
            corner_kernel,
            [parts[0].reshape(view), parts[1].reshape(view), parts[2].reshape(deep), parts[3].reshape(deep)],
            [(wide, jnp.float32), (wide, jnp.bfloat16), (narrow, jnp.bfloat16), (narrow, jnp.bfloat16)],
        )
        from_x = flipped(give_x, "group", 1)
        from_y = flipped(give_y, "gossip", 2)
        pairs = [(source, source ^ (2 * n_group + 1)) for source in range(replicas)]
        from_xy = lax.ppermute(give_xy, ("gossip", "group"), pairs)
        shape = (own_rows, dout)
        others = [(shape, jnp.bfloat16)] * (lead - 1)
        keep, *gives = call(spread_kernel, [keep, from_y, from_x, from_xy], [(shape, jnp.float32)] + others)
        gots = []
        for other, give in enumerate(gives, 1):
            gots.append(flipped(give, "gossip", 4 * other))
        (mean_weights,) = call(functools.partial(mean_kernel, replicas), [keep] + gots, [(shape, jnp.float32)])
    else:
        mean_weights = scattered_sum(jnp.concatenate(parts, axis=1)) / replicas
    (replica_weights,) = call(finish_kernel, [plan] + last, [((din, dout), jnp.bfloat16)])
    return (replica_weights[None], mean_weights)


def solution(mesh):
    return jax.shard_map(
        steps,
        mesh=mesh,
        in_specs=(
            P(("gossip", "group"), None, None),
            P(("gossip", "group"), None),
            P(("gossip", "group"), None),
            P(),
            P(("gossip", "group"), None),
        ),
        out_specs=(P(("gossip", "group"), None, None), P(("gossip", "group"), None)),
        check_vma=False,
    )
```

```python
import functools
import math

import jax
import jax.numpy as jnp
from jax import lax
from jax.experimental import pallas as pl
from jax.experimental.pallas import tpu as pltpu
from jax.sharding import PartitionSpec as P


STEPS = 3
HALVES = 2
KERNEL_VMEM = 20 << 20

learning_rate = 0.3
momentum_decay = 0.9


def shifted(value, axis, steps):
    count = lax.axis_size(axis)
    pairs = [(source, (source + steps) % count) for source in range(count)]
    return lax.ppermute(value, axis, pairs)


def flipped(value, axis, bit):
    count = lax.axis_size(axis)
    return lax.ppermute(value, axis, [(source, source ^ bit) for source in range(count)])


def shares(plan_ref, step):
    own = plan_ref[step, 0].astype(jnp.float32)
    peer = plan_ref[step, 1].astype(jnp.float32)
    own, peer = jnp.full((1, 1), own), jnp.full((1, 1), peer)
    return own / (own + peer), peer / (own + peer)


def gradient_of(batch_in, batch_out, rounded):
    fan_scale = 1.0 / math.sqrt(batch_in.shape[1])
    preact = jnp.dot(batch_in, rounded, preferred_element_type=jnp.float32) * fan_scale
    normal_cdf = 0.5 * (1.0 + lax.erf(preact * (1.0 / math.sqrt(2.0))))
    normal_pdf = jnp.exp(-0.5 * preact * preact) * (1.0 / math.sqrt(2.0 * math.pi))
    residual = preact * normal_cdf - batch_out.astype(jnp.float32)
    derivative = normal_cdf + preact * normal_pdf
    delta = (residual * derivative).astype(jnp.bfloat16)
    product = lax.dot_general(
        batch_in, delta, (((0,), (0,)), ((), ())), preferred_element_type=jnp.float32
    )
    return product * fan_scale


def shard_of(order, x, t, step, columns):
    batch = x.shape[0] // STEPS
    rows = pl.ds(pl.multiple_of(order[0, step] * batch, batch), batch)
    return x[rows, :], t[rows, columns]


def first_kernel(order, plan, x, t, *refs):
    own, _ = shares(plan, 0)
    weights, outs = refs[:HALVES], refs[HALVES:]
    width = weights[0].shape[1]
    for half, w in enumerate(weights):
        base, velocity = outs[2 * half:2 * half + 2]
        columns = slice(half * width, (half + 1) * width)
        gradient = gradient_of(*shard_of(order, x, t, 0, columns), w[...])
        velocity[...] = gradient
        base[...] = own * w[...].astype(jnp.float32) - learning_rate * gradient


def middle_kernel(columns, order, plan, x, t, rounded, master, velocity_in, base, velocity):
    own, _ = shares(plan, 1)
    v = momentum_decay * velocity_in[...] + gradient_of(*shard_of(order, x, t, 1, columns), rounded[...])
    velocity[...] = v
    base[...] = own * master[...] - learning_rate * v


def last_kernel(columns, split, order, plan, x, t, rounded, master, velocity_in, base, *outs):
    own, last_peer = shares(plan, STEPS - 1)
    r = rounded[...]
    v = momentum_decay * velocity_in[...] + gradient_of(*shard_of(order, x, t, STEPS - 1, columns), r)
    b = own * master[...] - learning_rate * v
    base[...] = b
    part = b + last_peer * r.astype(jnp.float32)
    if not split:
        outs[0][...] = part
        return
    keep, give, held = outs
    held[...] = part.reshape(held.shape)
    mine = lax.axis_index("gossip") & 1
    keep[...] = held[:, pl.ds(mine, 1)].reshape(keep.shape)
    give[...] = held[:, pl.ds(1 - mine, 1)].reshape(give.shape)


def round_kernel(step, plan, base, arrived, rounded, master):
    _, peer = shares(plan, step)
    total = base[...] + peer * arrived[...].astype(jnp.float32)
    rounded[...] = total.astype(jnp.bfloat16)
    master[...] = total


def finish_kernel(plan, *refs):
    _, peer = shares(plan, STEPS - 1)
    out = refs[-1]
    width = out.shape[1] // HALVES
    for i in range(HALVES):
        base, arrived = refs[2 * i], refs[2 * i + 1]
        out[:, i * width:(i + 1) * width] = (base[...] + peer * arrived[...].astype(jnp.float32)).astype(jnp.bfloat16)


def leg_kernel(axis, bit, kept, arrived, keep, give):
    mine = (lax.axis_index(axis) >> bit) & 1
    for out, side in ((keep, mine), (give, 1 - mine)):
        at = pl.ds(side, 1)
        total = kept[:, at] + arrived[:, at].astype(jnp.float32)
        out[...] = total.reshape(out.shape).astype(out.dtype)


def corner_kernel(first, first_arrived, second, second_arrived, keep, give_y, give_x, give_xy):
    y, x = (lax.axis_index("gossip") >> 1) & 1, lax.axis_index("group") & 1
    width = first.shape[-1]
    for out, row in ((keep, y), (give_y, 1 - y)):
        at, column = pl.ds(row, 1), pl.ds(x, 1)
        total = first[:, at] + first_arrived[:, at].astype(jnp.float32)
        out[:, :, :width] = total.reshape(out.shape[:-1] + (width,)).astype(out.dtype)
        total = second[:, at, column] + second_arrived[:, at, column]
        out[:, :, width:] = total.reshape(out.shape[:-1] + (width,)).astype(out.dtype)
    for out, row in ((give_x, y), (give_xy, 1 - y)):
        at, column = pl.ds(row, 1), pl.ds(1 - x, 1)
        total = second[:, at, column] + second_arrived[:, at, column]
        out[...] = total.reshape(out.shape).astype(out.dtype)


def spread_kernel(kept, from_y, from_x, from_xy, keep, *gives):
    mine = lax.axis_index("gossip") >> 2
    width = from_x.shape[-1]
    for other, out in enumerate((keep,) + gives):
        at = pl.ds(mine ^ other, 1)
        rows = kept[at] + from_y[at].astype(jnp.float32)
        late = from_x[at].astype(jnp.float32) + from_xy[at].astype(jnp.float32)
        out[:, :width] = rows[:, :, :width].reshape(out.shape[0], width).astype(out.dtype)
        out[:, width:] = (rows[:, :, width:] + late).reshape(out.shape[0], width).astype(out.dtype)


def mean_kernel(replicas, keep, *refs):
    total = keep[...]
    for arrived in refs[:-1]:
        total = total + arrived[...].astype(jnp.float32)
    refs[-1][...] = total / replicas


def call(kernel, ins, outs, scratch=()):
    in_vmem, in_smem = pl.BlockSpec(memory_space=pltpu.VMEM), pl.BlockSpec(memory_space=pltpu.SMEM)
    return pl.pallas_call(
        kernel,
        in_specs=[in_smem if array.dtype == jnp.int32 else in_vmem for array in ins],
        out_specs=[in_vmem] * len(outs),
        out_shape=[jax.ShapeDtypeStruct(shape, dtype) for shape, dtype in outs],
        scratch_shapes=list(scratch),
        compiler_params=pltpu.CompilerParams(vmem_limit_bytes=KERNEL_VMEM),
    )(*ins)


def scattered_sum(value):
    n_gossip, n_group = lax.axis_size("gossip"), lax.axis_size("group")
    gossip_bits, group_bits = n_gossip.bit_length() - 1, n_group.bit_length() - 1
    rows = value.shape[0]
    value = value.reshape((2,) * (gossip_bits + group_bits) + (rows // (n_gossip * n_group), value.shape[1]))
    left = [("gossip", bit) for bit in reversed(range(gossip_bits))]
    left += [("group", bit) for bit in reversed(range(group_bits))]
    order = [("gossip", 0)] + [("group", bit) for bit in range(group_bits)]
    order += [("gossip", bit) for bit in range(1, gossip_bits)]
    for axis, bit in order:
        place = left.index((axis, bit))
        mine = (lax.axis_index(axis) >> bit) & 1
        keep = lax.dynamic_index_in_dim(value, mine, place, keepdims=False)
        give = lax.dynamic_index_in_dim(value, 1 - mine, place, keepdims=False)
        value = keep + flipped(give, axis, 1 << bit)
        left.pop(place)
    return value


def steps(weights, inputs, targets, plan, order):
    n_gossip, n_group = lax.axis_size("gossip"), lax.axis_size("group")
    replicas = n_gossip * n_group
    weights = weights[0]
    din, dout = weights.shape
    width = dout // HALVES
    own_rows = din // replicas
    split = own_rows % 16 == 0 and n_group == 2 and n_gossip % 4 == 0
    columns = [slice(half * width, (half + 1) * width) for half in range(HALVES)]
    half_f32, half_bf16 = ((din, width), jnp.float32), ((din, width), jnp.bfloat16)

    pieces, arrived0, rounds0, arrived1, middles = [], [], [], [], []
    for half in range(HALVES):
        pieces.append(weights[:, columns[half]])
        arrived0.append(shifted(pieces[half], "gossip", 1))
    firsts = call(first_kernel, [order, plan, inputs, targets] + pieces, [half_f32] * (2 * HALVES))
    for half in range(HALVES):
        rounds0.append(
            call(functools.partial(round_kernel, 0), [plan, firsts[2 * half], arrived0[half]], [half_bf16, half_f32])
        )
        arrived1.append(shifted(rounds0[half][0], "gossip", 2))
    for half in range(HALVES):
        middles.append(
            call(
                functools.partial(middle_kernel, columns[half]),
                [order, plan, inputs, targets] + list(rounds0[half]) + [firsts[2 * half + 1]],
                [half_f32] * 2,
            )
        )
    parts, last = [], []
    for half in range(HALVES):
        base1, velocity1 = middles[half]
        rounded2, master2 = call(
            functools.partial(round_kernel, 1), [plan, base1, arrived1[half]], [half_bf16, half_f32]
        )
        arrived2 = shifted(rounded2, "gossip", 4)
        outs, scratch = [half_f32] * 2, ()
        if split:
            pair = (n_gossip // 2, n_group * own_rows, width)
            outs = [half_f32, (pair, jnp.float32), (pair, jnp.float32)]
            scratch = (pltpu.VMEM((pair[0], 2) + pair[1:], jnp.float32),)
        base2, *part = call(
            functools.partial(last_kernel, columns[half], split),
            [order, plan, inputs, targets, rounded2, master2, velocity1],
            outs,
            scratch,
        )
        last += [base2, arrived2]
        if not split:
            parts.append(part[0])
            continue
        keep, give = part
        got = flipped(give, "gossip", 1)
        if half < HALVES - 1:
            view = (n_gossip // 2, n_group, own_rows, width)
            shape = (n_gossip // 2, own_rows, width)
            keep, give = call(
                functools.partial(leg_kernel, "group", 0),
                [keep.reshape(view), got.reshape(view)],
                [(shape, jnp.float32), (shape, jnp.bfloat16)],
            )
            got = flipped(give, "group", 1)
        parts += [keep, got]
    if split:
        lead = n_gossip // 4
        view = (lead, 2, own_rows, width)
        deep = (lead, 2, n_group, own_rows, width)
        wide, narrow = (lead, own_rows, dout), (lead, own_rows, width)
        keep, give_y, give_x, give_xy = call(
            corner_kernel,
            [parts[0].reshape(view), parts[1].reshape(view), parts[2].reshape(deep), parts[3].reshape(deep)],
            [(wide, jnp.float32), (wide, jnp.bfloat16), (narrow, jnp.bfloat16), (narrow, jnp.bfloat16)],
        )
        from_x = flipped(give_x, "group", 1)
        from_y = flipped(give_y, "gossip", 2)
        pairs = [(source, source ^ (2 * n_group + 1)) for source in range(replicas)]
        from_xy = lax.ppermute(give_xy, ("gossip", "group"), pairs)
        shape = (own_rows, dout)
        others = [(shape, jnp.bfloat16)] * (lead - 1)
        keep, *gives = call(spread_kernel, [keep, from_y, from_x, from_xy], [(shape, jnp.float32)] + others)
        gots = []
        for other, give in enumerate(gives, 1):
            gots.append(flipped(give, "gossip", 4 * other))
        (mean_weights,) = call(functools.partial(mean_kernel, replicas), [keep] + gots, [(shape, jnp.float32)])
    else:
        mean_weights = scattered_sum(jnp.concatenate(parts, axis=1)) / replicas
    (replica_weights,) = call(finish_kernel, [plan] + last, [((din, dout), jnp.bfloat16)])
    return (replica_weights[None], mean_weights)


def solution(mesh):
    return jax.shard_map(
        steps,
        mesh=mesh,
        in_specs=(
            P(("gossip", "group"), None, None),
            P(("gossip", "group"), None),
            P(("gossip", "group"), None),
            P(),
            P(("gossip", "group"), None),
        ),
        out_specs=(P(("gossip", "group"), None, None), P(("gossip", "group"), None)),
        check_vma=False,
    )
```

```python
import functools
import math

import jax
import jax.numpy as jnp
from jax import lax
from jax.experimental import pallas as pl
from jax.experimental.pallas import tpu as pltpu
from jax.sharding import PartitionSpec as P


STEPS = 3
HALVES = 2
KERNEL_VMEM = 20 << 20

learning_rate = 0.3
momentum_decay = 0.9


def shifted(value, axis, steps):
    count = lax.axis_size(axis)
    pairs = [(source, (source + steps) % count) for source in range(count)]
    return lax.ppermute(value, axis, pairs)


def flipped(value, axis, bit):
    count = lax.axis_size(axis)
    return lax.ppermute(value, axis, [(source, source ^ bit) for source in range(count)])


def shares(plan_ref, step):
    own = plan_ref[0, step].astype(jnp.float32)
    peer = plan_ref[1, step].astype(jnp.float32)
    own, peer = jnp.full((1, 1), own), jnp.full((1, 1), peer)
    return own / (own + peer), peer / (own + peer)


def gradient_of(batch_in, batch_out, rounded):
    fan_scale = 1.0 / math.sqrt(batch_in.shape[1])
    preact = jnp.dot(batch_in, rounded, preferred_element_type=jnp.float32) * fan_scale
    normal_cdf = 0.5 * (1.0 + lax.erf(preact * (1.0 / math.sqrt(2.0))))
    normal_pdf = jnp.exp(-0.5 * preact * preact) * (1.0 / math.sqrt(2.0 * math.pi))
    residual = preact * normal_cdf - batch_out.astype(jnp.float32)
    derivative = normal_cdf + preact * normal_pdf
    delta = (residual * derivative).astype(jnp.bfloat16)
    product = lax.dot_general(
        batch_in, delta, (((0,), (0,)), ((), ())), preferred_element_type=jnp.float32
    )
    return product * fan_scale


def shard_of(order, x, t, step, columns):
    batch = x.shape[0] // STEPS
    rows = pl.ds(pl.multiple_of(order[0, step] * batch, batch), batch)
    return x[rows, :], t[rows, columns]


def piece_kernel(half, weights, piece, sem):
    width = piece.shape[1]
    copy = pltpu.make_async_copy(weights.at[:, half * width:(half + 1) * width], piece, sem)
    copy.start()
    copy.wait()


def first_kernel(order, plan, x, t, *refs):
    own, _ = shares(plan, 0)
    weights, outs = refs[:HALVES], refs[HALVES:]
    width = weights[0].shape[1]
    for half, w in enumerate(weights):
        base, velocity = outs[2 * half:2 * half + 2]
        columns = slice(half * width, (half + 1) * width)
        gradient = gradient_of(*shard_of(order, x, t, 0, columns), w[...])
        velocity[...] = gradient
        base[...] = own * w[...].astype(jnp.float32) - learning_rate * gradient


def middle_kernel(columns, order, plan, x, t, rounded, master, velocity_in, base, velocity):
    own, _ = shares(plan, 1)
    v = momentum_decay * velocity_in[...] + gradient_of(*shard_of(order, x, t, 1, columns), rounded[...])
    velocity[...] = v
    base[...] = own * master[...] - learning_rate * v


def last_kernel(columns, split, order, plan, x, t, rounded, master, velocity_in, base, *outs):
    own, last_peer = shares(plan, STEPS - 1)
    r = rounded[...]
    v = momentum_decay * velocity_in[...] + gradient_of(*shard_of(order, x, t, STEPS - 1, columns), r)
    b = own * master[...] - learning_rate * v
    base[...] = b
    part = b + last_peer * r.astype(jnp.float32)
    if not split:
        outs[0][...] = part
        return
    keep, give, held = outs
    held[...] = part.reshape(held.shape)
    mine = lax.axis_index("gossip") & 1
    keep[...] = held[:, pl.ds(mine, 1)].reshape(keep.shape)
    give[...] = held[:, pl.ds(1 - mine, 1)].reshape(give.shape)


def round_kernel(step, plan, base, arrived, rounded, master):
    _, peer = shares(plan, step)
    total = base[...] + peer * arrived[...].astype(jnp.float32)
    rounded[...] = total.astype(jnp.bfloat16)
    master[...] = total


def final_weights(plan, base, arrived):
    _, peer = shares(plan, STEPS - 1)
    return (base[...] + peer * arrived[...].astype(jnp.float32)).astype(jnp.bfloat16)


def finish_kernel(plan, base, arrived, out):
    out[...] = final_weights(plan, base, arrived)


def final_kernel(replicas, plan, base, arrived, whole, *refs):
    del whole
    out = refs[-2] if replicas else refs[-1]
    out[...] = final_weights(plan, base, arrived)
    if replicas:
        total = refs[0][...]
        for piece in refs[1:-2]:
            total = total + piece[...].astype(jnp.float32)
        refs[-1][...] = total / replicas


def leg_kernel(axis, bit, kept, arrived, keep, give):
    mine = (lax.axis_index(axis) >> bit) & 1
    for out, side in ((keep, mine), (give, 1 - mine)):
        at = pl.ds(side, 1)
        total = kept[:, at] + arrived[:, at].astype(jnp.float32)
        out[...] = total.reshape(out.shape).astype(out.dtype)


def corner_kernel(first, first_arrived, second, second_arrived, keep, give_y, give_x, give_xy):
    y, x = (lax.axis_index("gossip") >> 1) & 1, lax.axis_index("group") & 1
    width = first.shape[-1]
    for out, row in ((keep, y), (give_y, 1 - y)):
        at, column = pl.ds(row, 1), pl.ds(x, 1)
        total = first[:, at] + first_arrived[:, at].astype(jnp.float32)
        out[:, :, :width] = total.reshape(out.shape[:-1] + (width,)).astype(out.dtype)
        total = second[:, at, column] + second_arrived[:, at, column]
        out[:, :, width:] = total.reshape(out.shape[:-1] + (width,)).astype(out.dtype)
    for out, row in ((give_x, y), (give_xy, 1 - y)):
        at, column = pl.ds(row, 1), pl.ds(1 - x, 1)
        total = second[:, at, column] + second_arrived[:, at, column]
        out[...] = total.reshape(out.shape).astype(out.dtype)


def spread_kernel(kept, from_y, from_x, from_xy, keep, *gives):
    mine = lax.axis_index("gossip") >> 2
    width = from_x.shape[-1]
    for other, out in enumerate((keep,) + gives):
        at = pl.ds(mine ^ other, 1)
        rows = kept[at] + from_y[at].astype(jnp.float32)
        late = from_x[at].astype(jnp.float32) + from_xy[at].astype(jnp.float32)
        out[:, :width] = rows[:, :, :width].reshape(out.shape[0], width).astype(out.dtype)
        out[:, width:] = (rows[:, :, width:] + late).reshape(out.shape[0], width).astype(out.dtype)


IN_VMEM = pl.BlockSpec(memory_space=pltpu.VMEM)
IN_SMEM = pl.BlockSpec(memory_space=pltpu.SMEM)


def call(kernel, ins, outs, scratch=(), out_specs=None, in_place=None, in_specs=None):
    in_specs = in_specs or [IN_SMEM if array.dtype == jnp.int32 else IN_VMEM for array in ins]
    aliases = {}
    if in_place is not None:
        in_specs[in_place] = pl.BlockSpec(memory_space=pl.ANY)
        aliases = {in_place: 0}
    return pl.pallas_call(
        kernel,
        grid=(1,) if out_specs else (),
        in_specs=in_specs,
        out_specs=out_specs or [IN_VMEM] * len(outs),
        out_shape=[jax.ShapeDtypeStruct(shape, dtype) for shape, dtype in outs],
        scratch_shapes=list(scratch),
        input_output_aliases=aliases,
        compiler_params=pltpu.CompilerParams(vmem_limit_bytes=KERNEL_VMEM),
    )(*ins)


def scattered_sum(value):
    n_gossip, n_group = lax.axis_size("gossip"), lax.axis_size("group")
    gossip_bits, group_bits = n_gossip.bit_length() - 1, n_group.bit_length() - 1
    rows = value.shape[0]
    value = value.reshape((2,) * (gossip_bits + group_bits) + (rows // (n_gossip * n_group), value.shape[1]))
    left = [("gossip", bit) for bit in reversed(range(gossip_bits))]
    left += [("group", bit) for bit in reversed(range(group_bits))]
    order = [("gossip", 0)] + [("group", bit) for bit in range(group_bits)]
    order += [("gossip", bit) for bit in range(1, gossip_bits)]
    for axis, bit in order:
        place = left.index((axis, bit))
        mine = (lax.axis_index(axis) >> bit) & 1
        keep = lax.dynamic_index_in_dim(value, mine, place, keepdims=False)
        give = lax.dynamic_index_in_dim(value, 1 - mine, place, keepdims=False)
        value = keep + flipped(give, axis, 1 << bit)
        left.pop(place)
    return value


def steps(weights, inputs, targets, plan, order):
    n_gossip, n_group = lax.axis_size("gossip"), lax.axis_size("group")
    replicas = n_gossip * n_group
    weights = weights[0]
    din, dout = weights.shape
    width = dout // HALVES
    own_rows = din // replicas
    split = own_rows % 16 == 0 and n_group == 2 and n_gossip % 4 == 0
    columns = [slice(half * width, (half + 1) * width) for half in range(HALVES)]
    half_f32, half_bf16 = ((din, width), jnp.float32), ((din, width), jnp.bfloat16)

    in_hbm = pltpu.with_memory_space_constraint(weights, pltpu.HBM)
    plan = plan.T
    pieces, arrived0, rounds0, arrived1, middles = [], [], [], [], []
    for half in range(HALVES):
        (piece,) = call(
            functools.partial(piece_kernel, half), [in_hbm], [half_bf16], (pltpu.SemaphoreType.DMA,),
            in_specs=[pl.BlockSpec(memory_space=pltpu.HBM)],
        )
        pieces.append(piece)
        arrived0.append(shifted(pieces[half], "gossip", 1))
    firsts = call(first_kernel, [order, plan, inputs, targets] + pieces, [half_f32] * (2 * HALVES))
    for half in range(HALVES):
        rounds0.append(
            call(functools.partial(round_kernel, 0), [plan, firsts[2 * half], arrived0[half]], [half_bf16, half_f32])
        )
        arrived1.append(shifted(rounds0[half][0], "gossip", 2))
    for half in range(HALVES):
        middles.append(
            call(
                functools.partial(middle_kernel, columns[half]),
                [order, plan, inputs, targets] + list(rounds0[half]) + [firsts[2 * half + 1]],
                [half_f32] * 2,
            )
        )
    parts, last = [], []
    for half in range(HALVES):
        base1, velocity1 = middles[half]
        rounded2, master2 = call(
            functools.partial(round_kernel, 1), [plan, base1, arrived1[half]], [half_bf16, half_f32]
        )
        arrived2 = shifted(rounded2, "gossip", 4)
        outs, scratch = [half_f32] * 2, ()
        if split:
            pair = (n_gossip // 2, n_group * own_rows, width)
            outs = [half_f32, (pair, jnp.float32), (pair, jnp.float32)]
            scratch = (pltpu.VMEM((pair[0], 2) + pair[1:], jnp.float32),)
        base2, *part = call(
            functools.partial(last_kernel, columns[half], split),
            [order, plan, inputs, targets, rounded2, master2, velocity1],
            outs,
            scratch,
        )
        last += [base2, arrived2]
        if not split:
            parts.append(part[0])
            continue
        keep, give = part
        got = flipped(give, "gossip", 1)
        if half < HALVES - 1:
            view = (n_gossip // 2, n_group, own_rows, width)
            shape = (n_gossip // 2, own_rows, width)
            keep, give = call(
                functools.partial(leg_kernel, "group", 0),
                [keep.reshape(view), got.reshape(view)],
                [(shape, jnp.float32), (shape, jnp.bfloat16)],
            )
            got = flipped(give, "group", 1)
        parts += [keep, got]
    if split:
        lead = n_gossip // 4
        view = (lead, 2, own_rows, width)
        deep = (lead, 2, n_group, own_rows, width)
        wide, narrow = (lead, own_rows, dout), (lead, own_rows, width)
        keep, give_y, give_x, give_xy = call(
            corner_kernel,
            [parts[0].reshape(view), parts[1].reshape(view), parts[2].reshape(deep), parts[3].reshape(deep)],
            [(wide, jnp.float32), (wide, jnp.bfloat16), (narrow, jnp.bfloat16), (narrow, jnp.bfloat16)],
        )
        from_x = flipped(give_x, "group", 1)
        from_y = flipped(give_y, "gossip", 2)
        pairs = [(source, source ^ (2 * n_group + 1)) for source in range(replicas)]
        from_xy = lax.ppermute(give_xy, ("gossip", "group"), pairs)
        shape = (own_rows, dout)
        others = [(shape, jnp.bfloat16)] * (lead - 1)
        keep, *gives = call(spread_kernel, [keep, from_y, from_x, from_xy], [(shape, jnp.float32)] + others)
        gots = []
        for other, give in enumerate(gives, 1):
            gots.append(flipped(give, "gossip", 4 * other))
    else:
        mean_weights = scattered_sum(jnp.concatenate(parts, axis=1)) / replicas
    result = ((din, dout), jnp.bfloat16)
    blocks = [pl.BlockSpec((din, width), lambda i, half=half: (0, half)) for half in range(HALVES)]
    (begun,) = call(finish_kernel, [plan] + last[:2], [result], out_specs=[blocks[0]])
    ins = [plan] + last[2:] + [begun]
    if split:
        replica_weights, mean_weights = call(
            functools.partial(final_kernel, replicas), ins + [keep] + gots, [result, (shape, jnp.float32)],
            out_specs=[blocks[1], IN_VMEM], in_place=3,
        )
    else:
        (replica_weights,) = call(
            functools.partial(final_kernel, None), ins, [result], out_specs=[blocks[1]], in_place=3
        )
    return (replica_weights[None], mean_weights)


def solution(mesh):
    return jax.shard_map(
        steps,
        mesh=mesh,
        in_specs=(
            P(("gossip", "group"), None, None),
            P(("gossip", "group"), None),
            P(("gossip", "group"), None),
            P(),
            P(("gossip", "group"), None),
        ),
        out_specs=(P(("gossip", "group"), None, None), P(("gossip", "group"), None)),
        check_vma=False,
    )
```

```python
import functools
import math

import jax
import jax.numpy as jnp
from jax import lax
from jax.experimental import pallas as pl
from jax.experimental.pallas import tpu as pltpu
from jax.sharding import PartitionSpec as P


STEPS = 3
HALVES = 2
KERNEL_VMEM = 20 << 20

learning_rate = 0.3
momentum_decay = 0.9


def shifted(value, axis, steps):
    count = lax.axis_size(axis)
    pairs = [(source, (source + steps) % count) for source in range(count)]
    return lax.ppermute(value, axis, pairs)


def flipped(value, axis, bit):
    count = lax.axis_size(axis)
    return lax.ppermute(value, axis, [(source, source ^ bit) for source in range(count)])


def shares(plan_ref, step):
    own = plan_ref[0, step].astype(jnp.float32)
    peer = plan_ref[1, step].astype(jnp.float32)
    own, peer = jnp.full((1, 1), own), jnp.full((1, 1), peer)
    return own / (own + peer), peer / (own + peer)


def gradient_of(batch_in, batch_out, rounded):
    fan_scale = 1.0 / math.sqrt(batch_in.shape[1])
    preact = jnp.dot(batch_in, rounded, preferred_element_type=jnp.float32) * fan_scale
    normal_cdf = 0.5 * (1.0 + lax.erf(preact * (1.0 / math.sqrt(2.0))))
    normal_pdf = jnp.exp(-0.5 * preact * preact) * (1.0 / math.sqrt(2.0 * math.pi))
    residual = preact * normal_cdf - batch_out.astype(jnp.float32)
    derivative = normal_cdf + preact * normal_pdf
    delta = (residual * derivative).astype(jnp.bfloat16)
    product = lax.dot_general(
        batch_in, delta, (((0,), (0,)), ((), ())), preferred_element_type=jnp.float32
    )
    return product * fan_scale


def shard_of(order, x, t, step, columns):
    batch = x.shape[0] // STEPS
    rows = pl.ds(pl.multiple_of(order[0, step] * batch, batch), batch)
    return x[rows, :], t[rows, columns]


def first_kernel(order, plan, x, t, *refs):
    own, _ = shares(plan, 0)
    weights, outs = refs[:HALVES], refs[HALVES:]
    width = weights[0].shape[1]
    for half, w in enumerate(weights):
        base, velocity = outs[2 * half:2 * half + 2]
        columns = slice(half * width, (half + 1) * width)
        gradient = gradient_of(*shard_of(order, x, t, 0, columns), w[...])
        velocity[...] = gradient
        base[...] = own * w[...].astype(jnp.float32) - learning_rate * gradient


def middle_kernel(columns, order, plan, x, t, rounded, master, velocity_in, base, velocity):
    own, _ = shares(plan, 1)
    v = momentum_decay * velocity_in[...] + gradient_of(*shard_of(order, x, t, 1, columns), rounded[...])
    velocity[...] = v
    base[...] = own * master[...] - learning_rate * v


def last_kernel(columns, split, order, plan, x, t, rounded, master, velocity_in, base, *outs):
    own, last_peer = shares(plan, STEPS - 1)
    r = rounded[...]
    v = momentum_decay * velocity_in[...] + gradient_of(*shard_of(order, x, t, STEPS - 1, columns), r)
    b = own * master[...] - learning_rate * v
    base[...] = b
    part = b + last_peer * r.astype(jnp.float32)
    if not split:
        outs[0][...] = part
        return
    keep, give, held = outs
    held[...] = part.reshape(held.shape)
    mine = lax.axis_index("gossip") & 1
    keep[...] = held[:, pl.ds(mine, 1)].reshape(keep.shape)
    give[...] = held[:, pl.ds(1 - mine, 1)].reshape(give.shape)


def round_kernel(step, plan, base, arrived, rounded, master):
    _, peer = shares(plan, step)
    total = base[...] + peer * arrived[...].astype(jnp.float32)
    rounded[...] = total.astype(jnp.bfloat16)
    master[...] = total


def finish_kernel(plan, base, arrived, *refs):
    _, peer = shares(plan, STEPS - 1)
    refs[-1][...] = (base[...] + peer * arrived[...].astype(jnp.float32)).astype(jnp.bfloat16)


def leg_kernel(axis, bit, kept, arrived, keep, give):
    mine = (lax.axis_index(axis) >> bit) & 1
    for out, side in ((keep, mine), (give, 1 - mine)):
        at = pl.ds(side, 1)
        total = kept[:, at] + arrived[:, at].astype(jnp.float32)
        out[...] = total.reshape(out.shape).astype(out.dtype)


def corner_kernel(first, first_arrived, second, second_arrived, keep, give_y, give_x, give_xy):
    y, x = (lax.axis_index("gossip") >> 1) & 1, lax.axis_index("group") & 1
    width = first.shape[-1]
    for out, row in ((keep, y), (give_y, 1 - y)):
        at, column = pl.ds(row, 1), pl.ds(x, 1)
        total = first[:, at] + first_arrived[:, at].astype(jnp.float32)
        out[:, :, :width] = total.reshape(out.shape[:-1] + (width,)).astype(out.dtype)
        total = second[:, at, column] + second_arrived[:, at, column]
        out[:, :, width:] = total.reshape(out.shape[:-1] + (width,)).astype(out.dtype)
    for out, row in ((give_x, y), (give_xy, 1 - y)):
        at, column = pl.ds(row, 1), pl.ds(1 - x, 1)
        total = second[:, at, column] + second_arrived[:, at, column]
        out[...] = total.reshape(out.shape).astype(out.dtype)


def spread_kernel(kept, from_y, from_x, from_xy, keep, *gives):
    mine = lax.axis_index("gossip") >> 2
    width = from_x.shape[-1]
    for other, out in enumerate((keep,) + gives):
        at = pl.ds(mine ^ other, 1)
        rows = kept[at] + from_y[at].astype(jnp.float32)
        late = from_x[at].astype(jnp.float32) + from_xy[at].astype(jnp.float32)
        out[:, :width] = rows[:, :, :width].reshape(out.shape[0], width).astype(out.dtype)
        out[:, width:] = (rows[:, :, width:] + late).reshape(out.shape[0], width).astype(out.dtype)


def mean_kernel(replicas, keep, *refs):
    total = keep[...]
    for piece in refs[:-1]:
        total = total + piece[...].astype(jnp.float32)
    refs[-1][...] = total / replicas


IN_VMEM = pl.BlockSpec(memory_space=pltpu.VMEM)
IN_SMEM = pl.BlockSpec(memory_space=pltpu.SMEM)


def call(kernel, ins, outs, scratch=(), out_specs=None, in_place=None):
    in_specs = [IN_SMEM if array.dtype == jnp.int32 else IN_VMEM for array in ins]
    aliases = {}
    if in_place is not None:
        in_specs[in_place] = pl.BlockSpec(memory_space=pl.ANY)
        aliases = {in_place: 0}
    return pl.pallas_call(
        kernel,
        grid=(1,) if out_specs else (),
        in_specs=in_specs,
        out_specs=out_specs or [IN_VMEM] * len(outs),
        out_shape=[jax.ShapeDtypeStruct(shape, dtype) for shape, dtype in outs],
        scratch_shapes=list(scratch),
        input_output_aliases=aliases,
        compiler_params=pltpu.CompilerParams(vmem_limit_bytes=KERNEL_VMEM),
    )(*ins)


def scattered_sum(value):
    n_gossip, n_group = lax.axis_size("gossip"), lax.axis_size("group")
    gossip_bits, group_bits = n_gossip.bit_length() - 1, n_group.bit_length() - 1
    rows = value.shape[0]
    value = value.reshape((2,) * (gossip_bits + group_bits) + (rows // (n_gossip * n_group), value.shape[1]))
    left = [("gossip", bit) for bit in reversed(range(gossip_bits))]
    left += [("group", bit) for bit in reversed(range(group_bits))]
    order = [("gossip", 0)] + [("group", bit) for bit in range(group_bits)]
    order += [("gossip", bit) for bit in range(1, gossip_bits)]
    for axis, bit in order:
        place = left.index((axis, bit))
        mine = (lax.axis_index(axis) >> bit) & 1
        keep = lax.dynamic_index_in_dim(value, mine, place, keepdims=False)
        give = lax.dynamic_index_in_dim(value, 1 - mine, place, keepdims=False)
        value = keep + flipped(give, axis, 1 << bit)
        left.pop(place)
    return value


def steps(weights, inputs, targets, plan, order):
    n_gossip, n_group = lax.axis_size("gossip"), lax.axis_size("group")
    replicas = n_gossip * n_group
    weights = weights[0]
    din, dout = weights.shape
    width = dout // HALVES
    own_rows = din // replicas
    split = own_rows % 16 == 0 and n_group == 2 and n_gossip % 4 == 0
    columns = [slice(half * width, (half + 1) * width) for half in range(HALVES)]
    half_f32, half_bf16 = ((din, width), jnp.float32), ((din, width), jnp.bfloat16)

    plan = plan.T
    pieces, arrived0, rounds0, arrived1, middles = [], [], [], [], []
    for half in range(HALVES):
        pieces.append(weights[:, columns[half]])
        weights = lax.optimization_barrier(weights)
        arrived0.append(shifted(pieces[half], "gossip", 1))
    firsts = call(first_kernel, [order, plan, inputs, targets] + pieces, [half_f32] * (2 * HALVES))
    for half in range(HALVES):
        rounds0.append(
            call(functools.partial(round_kernel, 0), [plan, firsts[2 * half], arrived0[half]], [half_bf16, half_f32])
        )
        arrived1.append(shifted(rounds0[half][0], "gossip", 2))
    for half in range(HALVES):
        middles.append(
            call(
                functools.partial(middle_kernel, columns[half]),
                [order, plan, inputs, targets] + list(rounds0[half]) + [firsts[2 * half + 1]],
                [half_f32] * 2,
            )
        )
    parts, last = [], []
    for half in range(HALVES):
        base1, velocity1 = middles[half]
        rounded2, master2 = call(
            functools.partial(round_kernel, 1), [plan, base1, arrived1[half]], [half_bf16, half_f32]
        )
        arrived2 = shifted(rounded2, "gossip", 4)
        outs, scratch = [half_f32] * 2, ()
        if split:
            pair = (n_gossip // 2, n_group * own_rows, width)
            outs = [half_f32, (pair, jnp.float32), (pair, jnp.float32)]
            scratch = (pltpu.VMEM((pair[0], 2) + pair[1:], jnp.float32),)
        base2, *part = call(
            functools.partial(last_kernel, columns[half], split),
            [order, plan, inputs, targets, rounded2, master2, velocity1],
            outs,
            scratch,
        )
        last += [base2, arrived2]
        if not split:
            parts.append(part[0])
            continue
        keep, give = part
        got = flipped(give, "gossip", 1)
        if half < HALVES - 1:
            view = (n_gossip // 2, n_group, own_rows, width)
            shape = (n_gossip // 2, own_rows, width)
            keep, give = call(
                functools.partial(leg_kernel, "group", 0),
                [keep.reshape(view), got.reshape(view)],
                [(shape, jnp.float32), (shape, jnp.bfloat16)],
            )
            got = flipped(give, "group", 1)
        parts += [keep, got]
    if split:
        lead = n_gossip // 4
        view = (lead, 2, own_rows, width)
        deep = (lead, 2, n_group, own_rows, width)
        wide, narrow = (lead, own_rows, dout), (lead, own_rows, width)
        keep, give_y, give_x, give_xy = call(
            corner_kernel,
            [parts[0].reshape(view), parts[1].reshape(view), parts[2].reshape(deep), parts[3].reshape(deep)],
            [(wide, jnp.float32), (wide, jnp.bfloat16), (narrow, jnp.bfloat16), (narrow, jnp.bfloat16)],
        )
        from_x = flipped(give_x, "group", 1)
        from_y = flipped(give_y, "gossip", 2)
        pairs = [(source, source ^ (2 * n_group + 1)) for source in range(replicas)]
        from_xy = lax.ppermute(give_xy, ("gossip", "group"), pairs)
        shape = (own_rows, dout)
        others = [(shape, jnp.bfloat16)] * (lead - 1)
        keep, *gives = call(spread_kernel, [keep, from_y, from_x, from_xy], [(shape, jnp.float32)] + others)
        gots = []
        for other, give in enumerate(gives, 1):
            gots.append(flipped(give, "gossip", 4 * other))
    else:
        mean_weights = scattered_sum(jnp.concatenate(parts, axis=1)) / replicas
    result, replica_weights = ((din, dout), jnp.bfloat16), []
    for half in range(HALVES):
        replica_weights = call(
            finish_kernel,
            [plan, *last[2 * half:2 * half + 2], *replica_weights],
            [result],
            out_specs=[pl.BlockSpec((din, width), lambda i, half=half: (0, half))],
            in_place=3 if half else None,
        )
    if split:
        (mean_weights,) = call(functools.partial(mean_kernel, replicas), [keep] + gots, [(shape, jnp.float32)])
    return (replica_weights[0][None], mean_weights)


def solution(mesh):
    return jax.shard_map(
        steps,
        mesh=mesh,
        in_specs=(
            P(("gossip", "group"), None, None),
            P(("gossip", "group"), None),
            P(("gossip", "group"), None),
            P(),
            P(("gossip", "group"), None),
        ),
        out_specs=(P(("gossip", "group"), None, None), P(("gossip", "group"), None)),
        check_vma=False,
    )
```

```python
import functools
import math

import jax
import jax.numpy as jnp
from jax import lax
from jax.experimental import pallas as pl
from jax.experimental.pallas import tpu as pltpu
from jax.sharding import PartitionSpec as P


STEPS = 3
HALVES = 2
KERNEL_VMEM = 20 << 20

learning_rate = 0.3
momentum_decay = 0.9


def shifted(value, axis, steps):
    count = lax.axis_size(axis)
    pairs = [(source, (source + steps) % count) for source in range(count)]
    return lax.ppermute(value, axis, pairs)


def flipped(value, axis, bit):
    count = lax.axis_size(axis)
    return lax.ppermute(value, axis, [(source, source ^ bit) for source in range(count)])


def shares(mix, step):
    return mix[2 * step:2 * step + 1, 0:1], mix[2 * step + 1:2 * step + 2, 0:1]


def gradient_of(batch_in, batch_out, rounded):
    fan_scale = 1.0 / math.sqrt(batch_in.shape[1])
    preact = jnp.dot(batch_in, rounded, preferred_element_type=jnp.float32) * fan_scale
    normal_cdf = 0.5 * (1.0 + lax.erf(preact * (1.0 / math.sqrt(2.0))))
    normal_pdf = jnp.exp(-0.5 * preact * preact) * (1.0 / math.sqrt(2.0 * math.pi))
    residual = preact * normal_cdf - batch_out.astype(jnp.float32)
    derivative = normal_cdf + preact * normal_pdf
    delta = (residual * derivative).astype(jnp.bfloat16)
    product = lax.dot_general(
        batch_in, delta, (((0,), (0,)), ((), ())), preferred_element_type=jnp.float32
    )
    return product * fan_scale


def first_kernel(order, plan, x, t, *refs):
    weights, (mix, *shards), outs = refs[:HALVES], refs[HALVES:HALVES + 2 * STEPS - 1], refs[HALVES + 2 * STEPS - 1:]
    batch = x.shape[0] // STEPS
    rows = [pl.ds(pl.multiple_of(order[0, step] * batch, batch), batch) for step in range(STEPS)]
    mix[...] = jnp.zeros_like(mix)
    for step in range(STEPS):
        own, peer = [jnp.full((1, mix.shape[1]), plan[i, step].astype(jnp.float32)) for i in range(2)]
        mix[2 * step:2 * step + 1, :] = own / (own + peer)
        mix[2 * step + 1:2 * step + 2, :] = peer / (own + peer)
    own, _ = shares(mix, 0)
    width = weights[0].shape[1]
    for half, w in enumerate(weights):
        base, velocity = outs[2 * half:2 * half + 2]
        columns = slice(half * width, (half + 1) * width)
        gradient = gradient_of(x[rows[0], :], t[rows[0], columns], w[...])
        velocity[...] = gradient
        base[...] = own * w[...].astype(jnp.float32) - learning_rate * gradient
    for step in range(1, STEPS):
        shards[2 * step - 2][...] = x[rows[step], :]
        shards[2 * step - 1][...] = t[rows[step], :]


def middle_kernel(columns, mix, x, t, rounded, master, velocity_in, base, velocity):
    own, _ = shares(mix, 1)
    v = momentum_decay * velocity_in[...] + gradient_of(x[...], t[:, columns], rounded[...])
    velocity[...] = v
    base[...] = own * master[...] - learning_rate * v


def last_kernel(columns, split, mix, x, t, rounded, master, velocity_in, base, *outs):
    own, last_peer = shares(mix, STEPS - 1)
    r = rounded[...]
    v = momentum_decay * velocity_in[...] + gradient_of(x[...], t[:, columns], r)
    b = own * master[...] - learning_rate * v
    base[...] = b
    part = b + last_peer * r.astype(jnp.float32)
    if not split:
        outs[0][...] = part
        return
    keep, give, held = outs
    held[...] = part.reshape(held.shape)
    mine = lax.axis_index("gossip") & 1
    keep[...] = held[:, pl.ds(mine, 1)].reshape(keep.shape)
    give[...] = held[:, pl.ds(1 - mine, 1)].reshape(give.shape)


def round_kernel(step, mix, base, arrived, rounded, master):
    _, peer = shares(mix, step)
    total = base[...] + peer * arrived[...].astype(jnp.float32)
    rounded[...] = total.astype(jnp.bfloat16)
    master[...] = total


def finish_kernel(mix, base, arrived, *refs):
    _, peer = shares(mix, STEPS - 1)
    refs[-1][...] = (base[...] + peer * arrived[...].astype(jnp.float32)).astype(jnp.bfloat16)


def leg_kernel(axis, bit, kept, arrived, keep, give):
    mine = (lax.axis_index(axis) >> bit) & 1
    for out, side in ((keep, mine), (give, 1 - mine)):
        at = pl.ds(side, 1)
        total = kept[:, at] + arrived[:, at].astype(jnp.float32)
        out[...] = total.reshape(out.shape).astype(out.dtype)


def corner_kernel(first, first_arrived, second, second_arrived, keep, give_y, give_x, give_xy):
    y, x = (lax.axis_index("gossip") >> 1) & 1, lax.axis_index("group") & 1
    width = first.shape[-1]
    for out, row in ((keep, y), (give_y, 1 - y)):
        at, column = pl.ds(row, 1), pl.ds(x, 1)
        total = first[:, at] + first_arrived[:, at].astype(jnp.float32)
        out[:, :, :width] = total.reshape(out.shape[:-1] + (width,)).astype(out.dtype)
        total = second[:, at, column] + second_arrived[:, at, column]
        out[:, :, width:] = total.reshape(out.shape[:-1] + (width,)).astype(out.dtype)
    for out, row in ((give_x, y), (give_xy, 1 - y)):
        at, column = pl.ds(row, 1), pl.ds(1 - x, 1)
        total = second[:, at, column] + second_arrived[:, at, column]
        out[...] = total.reshape(out.shape).astype(out.dtype)


def spread_kernel(kept, from_y, from_x, from_xy, keep, *gives):
    mine = lax.axis_index("gossip") >> 2
    width = from_x.shape[-1]
    for other, out in enumerate((keep,) + gives):
        at = pl.ds(mine ^ other, 1)
        rows = kept[at] + from_y[at].astype(jnp.float32)
        late = from_x[at].astype(jnp.float32) + from_xy[at].astype(jnp.float32)
        out[:, :width] = rows[:, :, :width].reshape(out.shape[0], width).astype(out.dtype)
        out[:, width:] = (rows[:, :, width:] + late).reshape(out.shape[0], width).astype(out.dtype)


def mean_kernel(replicas, keep, *refs):
    total = keep[...]
    for piece in refs[:-1]:
        total = total + piece[...].astype(jnp.float32)
    refs[-1][...] = total / replicas


IN_VMEM = pl.BlockSpec(memory_space=pltpu.VMEM)
IN_SMEM = pl.BlockSpec(memory_space=pltpu.SMEM)


def call(kernel, ins, outs, scratch=(), out_specs=None, in_place=None):
    in_specs = [IN_SMEM if array.dtype == jnp.int32 else IN_VMEM for array in ins]
    aliases = {}
    if in_place is not None:
        in_specs[in_place] = pl.BlockSpec(memory_space=pl.ANY)
        aliases = {in_place: 0}
    return pl.pallas_call(
        kernel,
        grid=(1,) if out_specs else (),
        in_specs=in_specs,
        out_specs=out_specs or [IN_VMEM] * len(outs),
        out_shape=[jax.ShapeDtypeStruct(shape, dtype) for shape, dtype in outs],
        scratch_shapes=list(scratch),
        input_output_aliases=aliases,
        compiler_params=pltpu.CompilerParams(vmem_limit_bytes=KERNEL_VMEM),
    )(*ins)


def scattered_sum(value):
    n_gossip, n_group = lax.axis_size("gossip"), lax.axis_size("group")
    gossip_bits, group_bits = n_gossip.bit_length() - 1, n_group.bit_length() - 1
    rows = value.shape[0]
    value = value.reshape((2,) * (gossip_bits + group_bits) + (rows // (n_gossip * n_group), value.shape[1]))
    left = [("gossip", bit) for bit in reversed(range(gossip_bits))]
    left += [("group", bit) for bit in reversed(range(group_bits))]
    order = [("gossip", 0)] + [("group", bit) for bit in range(group_bits)]
    order += [("gossip", bit) for bit in range(1, gossip_bits)]
    for axis, bit in order:
        place = left.index((axis, bit))
        mine = (lax.axis_index(axis) >> bit) & 1
        keep = lax.dynamic_index_in_dim(value, mine, place, keepdims=False)
        give = lax.dynamic_index_in_dim(value, 1 - mine, place, keepdims=False)
        value = keep + flipped(give, axis, 1 << bit)
        left.pop(place)
    return value


def steps(weights, inputs, targets, plan, order):
    n_gossip, n_group = lax.axis_size("gossip"), lax.axis_size("group")
    replicas = n_gossip * n_group
    weights = weights[0]
    din, dout = weights.shape
    width = dout // HALVES
    own_rows = din // replicas
    split = own_rows % 16 == 0 and n_group == 2 and n_gossip % 4 == 0
    columns = [slice(half * width, (half + 1) * width) for half in range(HALVES)]
    half_f32, half_bf16 = ((din, width), jnp.float32), ((din, width), jnp.bfloat16)

    plan = plan.T
    pieces, arrived0, rounds0, arrived1, middles = [], [], [], [], []
    for half in range(HALVES):
        pieces.append(weights[:, columns[half]])
        weights = lax.optimization_barrier(weights)
        arrived0.append(shifted(pieces[half], "gossip", 1))
    batch = inputs.shape[0] // STEPS
    shards = [((batch, din), inputs.dtype), ((batch, dout), targets.dtype)] * (STEPS - 1)
    outs = [((-(-2 * STEPS // 8) * 8, 128), jnp.float32)] + shards + [half_f32] * (2 * HALVES)
    mix, *rest = call(first_kernel, [order, plan, inputs, targets] + pieces, outs)
    shards, firsts = rest[:len(shards)], rest[len(shards):]
    for half in range(HALVES):
        rounds0.append(
            call(
                functools.partial(round_kernel, 0), [mix, firsts[2 * half], arrived0[half]], [half_bf16, half_f32]
            )
        )
        arrived1.append(shifted(rounds0[half][0], "gossip", 2))
    for half in range(HALVES):
        middles.append(
            call(
                functools.partial(middle_kernel, columns[half]),
                [mix] + shards[:2] + list(rounds0[half]) + [firsts[2 * half + 1]],
                [half_f32] * 2,
            )
        )
    parts, last = [], []
    for half in range(HALVES):
        base1, velocity1 = middles[half]
        rounded2, master2 = call(
            functools.partial(round_kernel, 1), [mix, base1, arrived1[half]], [half_bf16, half_f32]
        )
        arrived2 = shifted(rounded2, "gossip", 4)
        outs, scratch = [half_f32] * 2, ()
        if split:
            pair = (n_gossip // 2, n_group * own_rows, width)
            outs = [half_f32, (pair, jnp.float32), (pair, jnp.float32)]
            scratch = (pltpu.VMEM((pair[0], 2) + pair[1:], jnp.float32),)
        base2, *part = call(
            functools.partial(last_kernel, columns[half], split),
            [mix] + shards[2:] + [rounded2, master2, velocity1],
            outs,
            scratch,
        )
        last += [base2, arrived2]
        if not split:
            parts.append(part[0])
            continue
        keep, give = part
        got = flipped(give, "gossip", 1)
        if half < HALVES - 1:
            view = (n_gossip // 2, n_group, own_rows, width)
            shape = (n_gossip // 2, own_rows, width)
            keep, give = call(
                functools.partial(leg_kernel, "group", 0),
                [keep.reshape(view), got.reshape(view)],
                [(shape, jnp.float32), (shape, jnp.bfloat16)],
            )
            got = flipped(give, "group", 1)
        parts += [keep, got]
    if split:
        lead = n_gossip // 4
        view = (lead, 2, own_rows, width)
        deep = (lead, 2, n_group, own_rows, width)
        wide, narrow = (lead, own_rows, dout), (lead, own_rows, width)
        keep, give_y, give_x, give_xy = call(
            corner_kernel,
            [parts[0].reshape(view), parts[1].reshape(view), parts[2].reshape(deep), parts[3].reshape(deep)],
            [(wide, jnp.float32), (wide, jnp.bfloat16), (narrow, jnp.bfloat16), (narrow, jnp.bfloat16)],
        )
        from_x = flipped(give_x, "group", 1)
        from_y = flipped(give_y, "gossip", 2)
        pairs = [(source, source ^ (2 * n_group + 1)) for source in range(replicas)]
        from_xy = lax.ppermute(give_xy, ("gossip", "group"), pairs)
        shape = (own_rows, dout)
        others = [(shape, jnp.bfloat16)] * (lead - 1)
        keep, *gives = call(spread_kernel, [keep, from_y, from_x, from_xy], [(shape, jnp.float32)] + others)
        gots = []
        for other, give in enumerate(gives, 1):
            gots.append(flipped(give, "gossip", 4 * other))
    else:
        mean_weights = scattered_sum(jnp.concatenate(parts, axis=1)) / replicas
    result, replica_weights = ((din, dout), jnp.bfloat16), []
    for half in range(HALVES):
        replica_weights = call(
            finish_kernel,
            [mix, *last[2 * half:2 * half + 2], *replica_weights],
            [result],
            out_specs=[pl.BlockSpec((din, width), lambda i, half=half: (0, half))],
            in_place=3 if half else None,
        )
    if split:
        (mean_weights,) = call(functools.partial(mean_kernel, replicas), [keep] + gots, [(shape, jnp.float32)])
    return (replica_weights[0][None], mean_weights)


def solution(mesh):
    return jax.shard_map(
        steps,
        mesh=mesh,
        in_specs=(
            P(("gossip", "group"), None, None),
            P(("gossip", "group"), None),
            P(("gossip", "group"), None),
            P(),
            P(("gossip", "group"), None),
        ),
        out_specs=(P(("gossip", "group"), None, None), P(("gossip", "group"), None)),
        check_vma=False,
    )
```

```python
import functools
import math

import jax
import jax.numpy as jnp
from jax import lax
from jax.experimental import pallas as pl
from jax.experimental.pallas import tpu as pltpu
from jax.sharding import PartitionSpec as P


STEPS = 3
HALVES = 2
KERNEL_VMEM = 20 << 20

learning_rate = 0.3
momentum_decay = 0.9


def shifted(value, axis, steps):
    count = lax.axis_size(axis)
    pairs = [(source, (source + steps) % count) for source in range(count)]
    return lax.ppermute(value, axis, pairs)


def moved(value, target):
    count = lax.axis_size("gossip")
    pairs = [(source, target(source) % count) for source in range(count) if target(source) is not None]
    return lax.ppermute(value, "gossip", pairs)


def flipped(value, axis, bit):
    count = lax.axis_size(axis)
    return lax.ppermute(value, axis, [(source, source ^ bit) for source in range(count)])


def shares(mix, step):
    return mix[2 * step:2 * step + 1, 0:1], mix[2 * step + 1:2 * step + 2, 0:1]


def gradient_of(batch_in, batch_out, rounded):
    fan_scale = 1.0 / math.sqrt(batch_in.shape[1])
    preact = jnp.dot(batch_in, rounded, preferred_element_type=jnp.float32) * fan_scale
    normal_cdf = 0.5 * (1.0 + lax.erf(preact * (1.0 / math.sqrt(2.0))))
    normal_pdf = jnp.exp(-0.5 * preact * preact) * (1.0 / math.sqrt(2.0 * math.pi))
    residual = preact * normal_cdf - batch_out.astype(jnp.float32)
    derivative = normal_cdf + preact * normal_pdf
    delta = (residual * derivative).astype(jnp.bfloat16)
    product = lax.dot_general(
        batch_in, delta, (((0,), (0,)), ((), ())), preferred_element_type=jnp.float32
    )
    return product * fan_scale


def first_kernel(order, plan, x, t, weights, mix, *refs):
    shards, outs = refs[:2 * STEPS - 2], refs[2 * STEPS - 2:-4]
    x_first, t_first, w_held, arrivals = refs[-4:]
    shards = (x_first, t_first) + shards
    batch = x.shape[0] // STEPS
    copies = [pltpu.make_async_copy(weights, w_held, arrivals.at[2 * STEPS])]
    for step in range(STEPS):
        rows = pl.ds(pl.multiple_of(order[0, step] * batch, batch), batch)
        for i, source in enumerate((x, t)):
            at = 2 * step + i
            copies.append(pltpu.make_async_copy(source.at[rows, :], shards[at], arrivals.at[at]))
    for copy in copies:
        copy.start()
    mix[...] = jnp.zeros_like(mix)
    for step in range(STEPS):
        own, peer = [jnp.full((1, mix.shape[1]), plan[i, step].astype(jnp.float32)) for i in range(2)]
        mix[2 * step:2 * step + 1, :] = own / (own + peer)
        mix[2 * step + 1:2 * step + 2, :] = peer / (own + peer)
    own, _ = shares(mix, 0)
    width = weights.shape[1] // HALVES
    for copy in copies[:3]:
        copy.wait()
    for half in range(HALVES):
        base, velocity = outs[2 * half:2 * half + 2]
        columns = slice(half * width, (half + 1) * width)
        w = w_held[:, columns]
        gradient = gradient_of(x_first[...], t_first[:, columns], w)
        velocity[...] = gradient
        base[...] = own * w.astype(jnp.float32) - learning_rate * gradient
    for copy in copies[3:]:
        copy.wait()


def middle_kernel(columns, mix, x, t, rounded, master, velocity_in, base, velocity):
    own, _ = shares(mix, 1)
    v = momentum_decay * velocity_in[...] + gradient_of(x[...], t[:, columns], rounded[...])
    velocity[...] = v
    base[...] = own * master[...] - learning_rate * v


def last_kernel(columns, split, mix, x, t, rounded, master, velocity_in, base, *outs):
    own, last_peer = shares(mix, STEPS - 1)
    r = rounded[...]
    v = momentum_decay * velocity_in[...] + gradient_of(x[...], t[:, columns], r)
    b = own * master[...] - learning_rate * v
    base[...] = b
    part = b + last_peer * r.astype(jnp.float32)
    if not split:
        outs[0][...] = part
        return
    keep, give, held = outs
    held[...] = part.reshape(held.shape)
    mine = lax.axis_index("gossip") & 1
    keep[...] = held[:, pl.ds(mine, 1)].reshape(keep.shape)
    give[...] = held[:, pl.ds(1 - mine, 1)].reshape(give.shape)


def early_kernel(columns, mix, base, arrived, rounded):
    _, peer = shares(mix, 0)
    rounded[...] = (base[...] + peer * arrived[:, columns].astype(jnp.float32)).astype(jnp.bfloat16)


def round_kernel(step, columns, mix, base, core_0, core_1, rounded, master):
    _, peer = shares(mix, step)
    core = lax.axis_index("gossip") & 1

    def add(arrived):
        total = base[...] + peer * arrived[:, columns].astype(jnp.float32)
        rounded[...] = total.astype(jnp.bfloat16)
        master[...] = total

    pl.when(core == 0)(functools.partial(add, core_0))
    pl.when(core == 1)(functools.partial(add, core_1))


def finish_kernel(mix, base, arrived, *refs):
    _, peer = shares(mix, STEPS - 1)
    refs[-1][...] = (base[...] + peer * arrived[...].astype(jnp.float32)).astype(jnp.bfloat16)


def leg_kernel(axis, bit, kept, arrived, keep, give):
    mine = (lax.axis_index(axis) >> bit) & 1
    for out, side in ((keep, mine), (give, 1 - mine)):
        at = pl.ds(side, 1)
        total = kept[:, at] + arrived[:, at].astype(jnp.float32)
        out[...] = total.reshape(out.shape).astype(out.dtype)


def corner_kernel(first, first_arrived, second, second_arrived, keep, give_y, give_x, give_xy):
    y, x = (lax.axis_index("gossip") >> 1) & 1, lax.axis_index("group") & 1
    width = first.shape[-1]
    for out, row in ((keep, y), (give_y, 1 - y)):
        at, column = pl.ds(row, 1), pl.ds(x, 1)
        total = first[:, at] + first_arrived[:, at].astype(jnp.float32)
        out[:, :, :width] = total.reshape(out.shape[:-1] + (width,)).astype(out.dtype)
        total = second[:, at, column] + second_arrived[:, at, column]
        out[:, :, width:] = total.reshape(out.shape[:-1] + (width,)).astype(out.dtype)
    for out, row in ((give_x, y), (give_xy, 1 - y)):
        at, column = pl.ds(row, 1), pl.ds(1 - x, 1)
        total = second[:, at, column] + second_arrived[:, at, column]
        out[...] = total.reshape(out.shape).astype(out.dtype)


def spread_kernel(kept, from_y, from_x, from_xy, keep, *gives):
    mine = lax.axis_index("gossip") >> 2
    width = from_x.shape[-1]
    for other, out in enumerate((keep,) + gives):
        at = pl.ds(mine ^ other, 1)
        rows = kept[at] + from_y[at].astype(jnp.float32)
        late = from_x[at].astype(jnp.float32) + from_xy[at].astype(jnp.float32)
        out[:, :width] = rows[:, :, :width].reshape(out.shape[0], width).astype(out.dtype)
        out[:, width:] = (rows[:, :, width:] + late).reshape(out.shape[0], width).astype(out.dtype)


def mean_kernel(replicas, keep, *refs):
    total = keep[...]
    for piece in refs[:-1]:
        total = total + piece[...].astype(jnp.float32)
    refs[-1][...] = total / replicas


IN_VMEM = pl.BlockSpec(memory_space=pltpu.VMEM)
IN_SMEM = pl.BlockSpec(memory_space=pltpu.SMEM)


def call(kernel, ins, outs, scratch=(), out_specs=None, in_place=None, in_specs=None):
    in_specs = in_specs or [IN_SMEM if array.dtype == jnp.int32 else IN_VMEM for array in ins]
    aliases = {}
    if in_place is not None:
        in_specs[in_place] = pl.BlockSpec(memory_space=pl.ANY)
        aliases = {in_place: 0}
    return pl.pallas_call(
        kernel,
        grid=(1,) if out_specs else (),
        in_specs=in_specs,
        out_specs=out_specs or [IN_VMEM] * len(outs),
        out_shape=[jax.ShapeDtypeStruct(shape, dtype) for shape, dtype in outs],
        scratch_shapes=list(scratch),
        input_output_aliases=aliases,
        compiler_params=pltpu.CompilerParams(vmem_limit_bytes=KERNEL_VMEM),
    )(*ins)


def scattered_sum(value):
    n_gossip, n_group = lax.axis_size("gossip"), lax.axis_size("group")
    gossip_bits, group_bits = n_gossip.bit_length() - 1, n_group.bit_length() - 1
    rows = value.shape[0]
    value = value.reshape((2,) * (gossip_bits + group_bits) + (rows // (n_gossip * n_group), value.shape[1]))
    left = [("gossip", bit) for bit in reversed(range(gossip_bits))]
    left += [("group", bit) for bit in reversed(range(group_bits))]
    order = [("gossip", 0)] + [("group", bit) for bit in range(group_bits)]
    order += [("gossip", bit) for bit in range(1, gossip_bits)]
    for axis, bit in order:
        place = left.index((axis, bit))
        mine = (lax.axis_index(axis) >> bit) & 1
        keep = lax.dynamic_index_in_dim(value, mine, place, keepdims=False)
        give = lax.dynamic_index_in_dim(value, 1 - mine, place, keepdims=False)
        value = keep + flipped(give, axis, 1 << bit)
        left.pop(place)
    return value


def steps(weights, inputs, targets, plan, order):
    n_gossip, n_group = lax.axis_size("gossip"), lax.axis_size("group")
    replicas = n_gossip * n_group
    weights = weights[0]
    din, dout = weights.shape
    width = dout // HALVES
    own_rows = din // replicas
    split = own_rows % 16 == 0 and n_group == 2 and n_gossip % 4 == 0
    columns = [slice(half * width, (half + 1) * width) for half in range(HALVES)]
    half_f32, half_bf16 = ((din, width), jnp.float32), ((din, width), jnp.bfloat16)

    plan = plan.T
    leads, rounds0, arrived1, middles = [], [], [], []
    ship = moved(weights, lambda at: at + 1 if at & 1 else None)
    chip = moved(weights, lambda at: None if at & 1 else at + 1)
    batch = inputs.shape[0] // STEPS
    shards = [((batch, din), inputs.dtype), ((batch, dout), targets.dtype)] * (STEPS - 1)
    outs = [((-(-2 * STEPS // 8) * 8, 128), jnp.float32)] + shards + [half_f32] * (2 * HALVES)
    in_hbm = [pltpu.with_memory_space_constraint(array, pltpu.HBM) for array in (order, plan, inputs, targets, weights)]
    held = [pltpu.VMEM(*shard) for shard in shards[:2]] + [pltpu.VMEM(weights.shape, weights.dtype)]
    mix, *rest = call(
        first_kernel, in_hbm, outs, held + [pltpu.SemaphoreType.DMA((2 * STEPS + 1,))],
        in_specs=[IN_SMEM] * 2 + [pl.BlockSpec(memory_space=pltpu.HBM)] * 3,
    )
    shards, firsts = rest[:len(shards)], rest[len(shards):]
    for half in range(HALVES):
        (early,) = call(
            functools.partial(early_kernel, columns[half]), [mix, firsts[2 * half], chip], [half_bf16]
        )
        leads.append(moved(early, lambda at: at + 2 if at & 1 else None))
    for half in range(HALVES):
        rounds0.append(
            call(
                functools.partial(round_kernel, 0, columns[half]), [mix, firsts[2 * half], ship, chip],
                [half_bf16, half_f32],
            )
        )
        arrived1.append(moved(rounds0[half][0], lambda at: None if at & 1 else at + 2))
    for half in range(HALVES):
        middles.append(
            call(
                functools.partial(middle_kernel, columns[half]),
                [mix] + shards[:2] + list(rounds0[half]) + [firsts[2 * half + 1]],
                [half_f32] * 2,
            )
        )
    parts, last = [], []
    for half in range(HALVES):
        base1, velocity1 = middles[half]
        rounded2, master2 = call(
            functools.partial(round_kernel, 1, slice(None)), [mix, base1, arrived1[half], leads[half]],
            [half_bf16, half_f32],
        )
        arrived2 = shifted(rounded2, "gossip", 4)
        outs, scratch = [half_f32] * 2, ()
        if split:
            pair = (n_gossip // 2, n_group * own_rows, width)
            outs = [half_f32, (pair, jnp.float32), (pair, jnp.float32)]
            scratch = (pltpu.VMEM((pair[0], 2) + pair[1:], jnp.float32),)
        base2, *part = call(
            functools.partial(last_kernel, columns[half], split),
            [mix] + shards[2:] + [rounded2, master2, velocity1],
            outs,
            scratch,
        )
        last += [base2, arrived2]
        if not split:
            parts.append(part[0])
            continue
        keep, give = part
        got = flipped(give, "gossip", 1)
        if half < HALVES - 1:
            view = (n_gossip // 2, n_group, own_rows, width)
            shape = (n_gossip // 2, own_rows, width)
            keep, give = call(
                functools.partial(leg_kernel, "group", 0),
                [keep.reshape(view), got.reshape(view)],
                [(shape, jnp.float32), (shape, jnp.bfloat16)],
            )
            got = flipped(give, "group", 1)
        parts += [keep, got]
    if split:
        lead = n_gossip // 4
        view = (lead, 2, own_rows, width)
        deep = (lead, 2, n_group, own_rows, width)
        wide, narrow = (lead, own_rows, dout), (lead, own_rows, width)
        keep, give_y, give_x, give_xy = call(
            corner_kernel,
            [parts[0].reshape(view), parts[1].reshape(view), parts[2].reshape(deep), parts[3].reshape(deep)],
            [(wide, jnp.float32), (wide, jnp.bfloat16), (narrow, jnp.bfloat16), (narrow, jnp.bfloat16)],
        )
        from_x = flipped(give_x, "group", 1)
        from_y = flipped(give_y, "gossip", 2)
        pairs = [(source, source ^ (2 * n_group + 1)) for source in range(replicas)]
        from_xy = lax.ppermute(give_xy, ("gossip", "group"), pairs)
        shape = (own_rows, dout)
        others = [(shape, jnp.bfloat16)] * (lead - 1)
        keep, *gives = call(spread_kernel, [keep, from_y, from_x, from_xy], [(shape, jnp.float32)] + others)
        gots = []
        for other, give in enumerate(gives, 1):
            gots.append(flipped(give, "gossip", 4 * other))
    else:
        mean_weights = scattered_sum(jnp.concatenate(parts, axis=1)) / replicas
    result, replica_weights = ((din, dout), jnp.bfloat16), []
    for half in range(HALVES):
        replica_weights = call(
            finish_kernel,
            [mix, *last[2 * half:2 * half + 2], *replica_weights],
            [result],
            out_specs=[pl.BlockSpec((din, width), lambda i, half=half: (0, half))],
            in_place=3 if half else None,
        )
    if split:
        (mean_weights,) = call(functools.partial(mean_kernel, replicas), [keep] + gots, [(shape, jnp.float32)])
    return (replica_weights[0][None], mean_weights)


def solution(mesh):
    return jax.shard_map(
        steps,
        mesh=mesh,
        in_specs=(
            P(("gossip", "group"), None, None),
            P(("gossip", "group"), None),
            P(("gossip", "group"), None),
            P(),
            P(("gossip", "group"), None),
        ),
        out_specs=(P(("gossip", "group"), None, None), P(("gossip", "group"), None)),
        check_vma=False,
    )
```

```python
import functools
import math

import jax
import jax.numpy as jnp
from jax import lax
from jax.experimental import pallas as pl
from jax.experimental.pallas import tpu as pltpu
from jax.sharding import PartitionSpec as P


STEPS = 3
HALVES = 2
KERNEL_VMEM = 20 << 20

learning_rate = 0.3
momentum_decay = 0.9


def shifted(value, axis, steps):
    count = lax.axis_size(axis)
    pairs = [(source, (source + steps) % count) for source in range(count)]
    return lax.ppermute(value, axis, pairs)


def moved(value, target):
    count = lax.axis_size("gossip")
    pairs = [(source, target(source) % count) for source in range(count) if target(source) is not None]
    return lax.ppermute(value, "gossip", pairs)


def flipped(value, axis, bit):
    count = lax.axis_size(axis)
    return lax.ppermute(value, axis, [(source, source ^ bit) for source in range(count)])


def shares(mix, step):
    return mix[2 * step:2 * step + 1, 0:1], mix[2 * step + 1:2 * step + 2, 0:1]


def gradient_of(batch_in, batch_out, rounded):
    fan_scale = 1.0 / math.sqrt(batch_in.shape[1])
    preact = jnp.dot(batch_in, rounded, preferred_element_type=jnp.float32) * fan_scale
    normal_cdf = 0.5 * (1.0 + lax.erf(preact * (1.0 / math.sqrt(2.0))))
    normal_pdf = jnp.exp(-0.5 * preact * preact) * (1.0 / math.sqrt(2.0 * math.pi))
    residual = preact * normal_cdf - batch_out.astype(jnp.float32)
    derivative = normal_cdf + preact * normal_pdf
    delta = (residual * derivative).astype(jnp.bfloat16)
    product = lax.dot_general(
        batch_in, delta, (((0,), (0,)), ((), ())), preferred_element_type=jnp.float32
    )
    return product * fan_scale


def first_kernel(order, plan, x, t, *refs):
    weights, (mix, *shards), outs = refs[:HALVES], refs[HALVES:HALVES + 2 * STEPS - 1], refs[HALVES + 2 * STEPS - 1:]
    batch = x.shape[0] // STEPS
    rows = [pl.ds(pl.multiple_of(order[0, step] * batch, batch), batch) for step in range(STEPS)]
    mix[...] = jnp.zeros_like(mix)
    for step in range(STEPS):
        own, peer = [jnp.full((1, mix.shape[1]), plan[i, step].astype(jnp.float32)) for i in range(2)]
        mix[2 * step:2 * step + 1, :] = own / (own + peer)
        mix[2 * step + 1:2 * step + 2, :] = peer / (own + peer)
    own, _ = shares(mix, 0)
    width = weights[0].shape[1]
    for half, w in enumerate(weights):
        base, velocity = outs[2 * half:2 * half + 2]
        columns = slice(half * width, (half + 1) * width)
        gradient = gradient_of(x[rows[0], :], t[rows[0], columns], w[...])
        velocity[...] = gradient
        base[...] = own * w[...].astype(jnp.float32) - learning_rate * gradient
    for step in range(1, STEPS):
        shards[2 * step - 2][...] = x[rows[step], :]
        shards[2 * step - 1][...] = t[rows[step], :]


def middle_kernel(columns, mix, x, t, rounded, master, velocity_in, base, velocity):
    own, _ = shares(mix, 1)
    v = momentum_decay * velocity_in[...] + gradient_of(x[...], t[:, columns], rounded[...])
    velocity[...] = v
    base[...] = own * master[...] - learning_rate * v


def last_kernel(columns, split, mix, x, t, rounded, master, velocity_in, base, *outs):
    own, last_peer = shares(mix, STEPS - 1)
    r = rounded[...]
    v = momentum_decay * velocity_in[...] + gradient_of(x[...], t[:, columns], r)
    b = own * master[...] - learning_rate * v
    base[...] = b
    part = b + last_peer * r.astype(jnp.float32)
    if not split:
        outs[0][...] = part
        return
    keep, give, held = outs
    held[...] = part.reshape(held.shape)
    mine = lax.axis_index("gossip") & 1
    keep[...] = held[:, pl.ds(mine, 1)].reshape(keep.shape)
    give[...] = held[:, pl.ds(1 - mine, 1)].reshape(give.shape)


def round_kernel(step, mix, base, arrived, rounded, master, *pieces):
    _, peer = shares(mix, step)
    total = base[...] + peer * arrived[...].astype(jnp.float32)
    rounded[...] = total.astype(jnp.bfloat16)
    master[...] = total
    for i, piece in enumerate(pieces):
        width = piece.shape[1]
        piece[...] = rounded[:, i * width:(i + 1) * width]


def gather_kernel(step, mix, base, direct, hop, relay, lead, rounded, master):
    _, peer = shares(mix, step)
    at = lax.axis_index("gossip")
    core, chip = at & 1, (at >> 1) & 1

    def add(columns, arrived):
        total = base[:, columns] + peer * arrived[...].astype(jnp.float32)
        rounded[:, columns] = total.astype(jnp.bfloat16)
        master[:, columns] = total

    width = hop.shape[1]
    pl.when(core == 0)(lambda: add(slice(None), direct))
    pl.when((core == 1) & (chip == 1))(lambda: add(slice(0, width), hop))
    pl.when((core == 1) & (chip == 0))(lambda: add(slice(0, width), relay))
    pl.when(core == 1)(lambda: add(slice(width, None), lead))


def finish_kernel(count, mix, base, *refs):
    _, peer = shares(mix, STEPS - 1)
    core = lax.axis_index("gossip") & 1

    def add(arrived):
        refs[-1][...] = (base[...] + peer * arrived[...].astype(jnp.float32)).astype(jnp.bfloat16)

    if count == 1:
        add(refs[0])
    else:
        for i in range(count):
            pl.when(core == i)(functools.partial(add, refs[i]))


def leg_kernel(axis, bit, kept, arrived, keep, give):
    mine = (lax.axis_index(axis) >> bit) & 1
    for out, side in ((keep, mine), (give, 1 - mine)):
        at = pl.ds(side, 1)
        total = kept[:, at] + arrived[:, at].astype(jnp.float32)
        out[...] = total.reshape(out.shape).astype(out.dtype)


def corner_kernel(first, first_arrived, second, second_arrived, keep, give_y, give_x, give_xy):
    y, x = (lax.axis_index("gossip") >> 1) & 1, lax.axis_index("group") & 1
    width = first.shape[-1]
    for out, row in ((keep, y), (give_y, 1 - y)):
        at, column = pl.ds(row, 1), pl.ds(x, 1)
        total = first[:, at] + first_arrived[:, at].astype(jnp.float32)
        out[:, :, :width] = total.reshape(out.shape[:-1] + (width,)).astype(out.dtype)
        total = second[:, at, column] + second_arrived[:, at, column]
        out[:, :, width:] = total.reshape(out.shape[:-1] + (width,)).astype(out.dtype)
    for out, row in ((give_x, y), (give_xy, 1 - y)):
        at, column = pl.ds(row, 1), pl.ds(1 - x, 1)
        total = second[:, at, column] + second_arrived[:, at, column]
        out[...] = total.reshape(out.shape).astype(out.dtype)


def spread_kernel(kept, from_y, from_x, from_xy, keep, *gives):
    mine = lax.axis_index("gossip") >> 2
    width = from_x.shape[-1]
    for other, out in enumerate((keep,) + gives):
        at = pl.ds(mine ^ other, 1)
        rows = kept[at] + from_y[at].astype(jnp.float32)
        late = from_x[at].astype(jnp.float32) + from_xy[at].astype(jnp.float32)
        out[:, :width] = rows[:, :, :width].reshape(out.shape[0], width).astype(out.dtype)
        out[:, width:] = (rows[:, :, width:] + late).reshape(out.shape[0], width).astype(out.dtype)


def mean_kernel(replicas, keep, *refs):
    total = keep[...]
    for piece in refs[:-1]:
        total = total + piece[...].astype(jnp.float32)
    refs[-1][...] = total / replicas


IN_VMEM = pl.BlockSpec(memory_space=pltpu.VMEM)
IN_SMEM = pl.BlockSpec(memory_space=pltpu.SMEM)


def call(kernel, ins, outs, scratch=(), out_specs=None, in_place=None):
    in_specs = [IN_SMEM if array.dtype == jnp.int32 else IN_VMEM for array in ins]
    aliases = {}
    if in_place is not None:
        in_specs[in_place] = pl.BlockSpec(memory_space=pl.ANY)
        aliases = {in_place: 0}
    return pl.pallas_call(
        kernel,
        grid=(1,) if out_specs else (),
        in_specs=in_specs,
        out_specs=out_specs or [IN_VMEM] * len(outs),
        out_shape=[jax.ShapeDtypeStruct(shape, dtype) for shape, dtype in outs],
        scratch_shapes=list(scratch),
        input_output_aliases=aliases,
        compiler_params=pltpu.CompilerParams(vmem_limit_bytes=KERNEL_VMEM),
    )(*ins)


def scattered_sum(value):
    n_gossip, n_group = lax.axis_size("gossip"), lax.axis_size("group")
    gossip_bits, group_bits = n_gossip.bit_length() - 1, n_group.bit_length() - 1
    rows = value.shape[0]
    value = value.reshape((2,) * (gossip_bits + group_bits) + (rows // (n_gossip * n_group), value.shape[1]))
    left = [("gossip", bit) for bit in reversed(range(gossip_bits))]
    left += [("group", bit) for bit in reversed(range(group_bits))]
    order = [("gossip", 0)] + [("group", bit) for bit in range(group_bits)]
    order += [("gossip", bit) for bit in range(1, gossip_bits)]
    for axis, bit in order:
        place = left.index((axis, bit))
        mine = (lax.axis_index(axis) >> bit) & 1
        keep = lax.dynamic_index_in_dim(value, mine, place, keepdims=False)
        give = lax.dynamic_index_in_dim(value, 1 - mine, place, keepdims=False)
        value = keep + flipped(give, axis, 1 << bit)
        left.pop(place)
    return value


def steps(weights, inputs, targets, plan, order):
    n_gossip, n_group = lax.axis_size("gossip"), lax.axis_size("group")
    replicas = n_gossip * n_group
    weights = weights[0]
    din, dout = weights.shape
    width = dout // HALVES
    own_rows = din // replicas
    split = own_rows % 16 == 0 and n_group == 2 and n_gossip % 4 == 0
    columns = [slice(half * width, (half + 1) * width) for half in range(HALVES)]
    half_f32, half_bf16 = ((din, width), jnp.float32), ((din, width), jnp.bfloat16)

    plan = plan.T
    pieces, arrived0, rounds0, arrived1, middles = [], [], [], [], []
    for half in range(HALVES):
        pieces.append(weights[:, columns[half]])
        weights = lax.optimization_barrier(weights)
        arrived0.append(shifted(pieces[half], "gossip", 1))
    batch = inputs.shape[0] // STEPS
    shards = [((batch, din), inputs.dtype), ((batch, dout), targets.dtype)] * (STEPS - 1)
    outs = [((-(-2 * STEPS // 8) * 8, 128), jnp.float32)] + shards + [half_f32] * (2 * HALVES)
    mix, *rest = call(first_kernel, [order, plan, inputs, targets] + pieces, outs)
    shards, firsts = rest[:len(shards)], rest[len(shards):]
    for half in range(HALVES):
        quarter, extra = width // 2, half == HALVES - 1
        outs = [half_bf16, half_f32] + [((din, quarter), jnp.bfloat16)] * (2 * extra)
        rounded, master, *quarters = call(
            functools.partial(round_kernel, 0), [mix, firsts[2 * half], arrived0[half]], outs
        )
        rounds0.append((rounded, master))
        if not extra:
            arrived1.append([shifted(rounded, "gossip", 2)])
            continue
        hop = moved(quarters[0], lambda at: at ^ 2 if at & 1 else None)
        lead = moved(quarters[1], lambda at: at + 2 if at & 1 else None)
        direct = moved(rounded, lambda at: None if at & 1 else at + 2)
    for half in range(HALVES):
        middles.append(
            call(
                functools.partial(middle_kernel, columns[half]),
                [mix] + shards[:2] + list(rounds0[half]) + [firsts[2 * half + 1]],
                [half_f32] * 2,
            )
        )
    parts, last = [], []
    for half in range(HALVES):
        base1, velocity1 = middles[half]
        kernel = round_kernel if half < HALVES - 1 else gather_kernel
        rounded2, master2 = call(
            functools.partial(kernel, 1), [mix, base1] + arrived1[half], [half_bf16, half_f32]
        )
        if half < HALVES - 1:
            core_0 = moved(rounded2, lambda at: None if at & 1 else at + 4)
            relay = moved(hop, lambda at: at + 4 if at & 3 == 1 else None)
            arrived1.append([direct, hop, relay, lead])
            core_1 = moved(rounded2, lambda at: at + 4 if at & 1 else None)
            arrived2 = [core_0, core_1]
        else:
            arrived2 = [shifted(rounded2, "gossip", 4)]
        outs, scratch = [half_f32] * 2, ()
        if split:
            pair = (n_gossip // 2, n_group * own_rows, width)
            outs = [half_f32, (pair, jnp.float32), (pair, jnp.float32)]
            scratch = (pltpu.VMEM((pair[0], 2) + pair[1:], jnp.float32),)
        base2, *part = call(
            functools.partial(last_kernel, columns[half], split),
            [mix] + shards[2:] + [rounded2, master2, velocity1],
            outs,
            scratch,
        )
        last.append([base2] + arrived2)
        if not split:
            parts.append(part[0])
            continue
        keep, give = part
        got = flipped(give, "gossip", 1)
        if half < HALVES - 1:
            view = (n_gossip // 2, n_group, own_rows, width)
            shape = (n_gossip // 2, own_rows, width)
            keep, give = call(
                functools.partial(leg_kernel, "group", 0),
                [keep.reshape(view), got.reshape(view)],
                [(shape, jnp.float32), (shape, jnp.bfloat16)],
            )
            got = flipped(give, "group", 1)
        parts += [keep, got]
    if split:
        lead = n_gossip // 4
        view = (lead, 2, own_rows, width)
        deep = (lead, 2, n_group, own_rows, width)
        wide, narrow = (lead, own_rows, dout), (lead, own_rows, width)
        keep, give_y, give_x, give_xy = call(
            corner_kernel,
            [parts[0].reshape(view), parts[1].reshape(view), parts[2].reshape(deep), parts[3].reshape(deep)],
            [(wide, jnp.float32), (wide, jnp.bfloat16), (narrow, jnp.bfloat16), (narrow, jnp.bfloat16)],
        )
        from_x = flipped(give_x, "group", 1)
        from_y = flipped(give_y, "gossip", 2)
        pairs = [(source, source ^ (2 * n_group + 1)) for source in range(replicas)]
        from_xy = lax.ppermute(give_xy, ("gossip", "group"), pairs)
        shape = (own_rows, dout)
        others = [(shape, jnp.bfloat16)] * (lead - 1)
        keep, *gives = call(spread_kernel, [keep, from_y, from_x, from_xy], [(shape, jnp.float32)] + others)
        gots = []
        for other, give in enumerate(gives, 1):
            gots.append(flipped(give, "gossip", 4 * other))
    else:
        mean_weights = scattered_sum(jnp.concatenate(parts, axis=1)) / replicas
    result, replica_weights = ((din, dout), jnp.bfloat16), []
    for half in range(HALVES):
        ins = [mix] + last[half] + list(replica_weights)
        replica_weights = call(
            functools.partial(finish_kernel, len(last[half]) - 1),
            ins,
            [result],
            out_specs=[pl.BlockSpec((din, width), lambda i, half=half: (0, half))],
            in_place=len(ins) - 1 if half else None,
        )
    if split:
        (mean_weights,) = call(functools.partial(mean_kernel, replicas), [keep] + gots, [(shape, jnp.float32)])
    return (replica_weights[0][None], mean_weights)


def solution(mesh):
    return jax.shard_map(
        steps,
        mesh=mesh,
        in_specs=(
            P(("gossip", "group"), None, None),
            P(("gossip", "group"), None),
            P(("gossip", "group"), None),
            P(),
            P(("gossip", "group"), None),
        ),
        out_specs=(P(("gossip", "group"), None, None), P(("gossip", "group"), None)),
        check_vma=False,
    )
```

```python
import functools
import math

import jax
import jax.numpy as jnp
from jax import lax
from jax.experimental import pallas as pl
from jax.experimental.pallas import tpu as pltpu
from jax.sharding import PartitionSpec as P


STEPS = 3
HALVES = 2
KERNEL_VMEM = 20 << 20

learning_rate = 0.3
momentum_decay = 0.9


def shifted(value, axis, steps):
    count = lax.axis_size(axis)
    pairs = [(source, (source + steps) % count) for source in range(count)]
    return lax.ppermute(value, axis, pairs)


def flipped(value, axis, bit):
    count = lax.axis_size(axis)
    return lax.ppermute(value, axis, [(source, source ^ bit) for source in range(count)])


def shares(mix, step):
    return mix[2 * step:2 * step + 1, 0:1], mix[2 * step + 1:2 * step + 2, 0:1]


def gradient_of(batch_in, batch_out, rounded):
    fan_scale = 1.0 / math.sqrt(batch_in.shape[1])
    preact = jnp.dot(batch_in, rounded, preferred_element_type=jnp.float32) * fan_scale
    normal_cdf = 0.5 * (1.0 + lax.erf(preact * (1.0 / math.sqrt(2.0))))
    normal_pdf = jnp.exp(-0.5 * preact * preact) * (1.0 / math.sqrt(2.0 * math.pi))
    residual = preact * normal_cdf - batch_out.astype(jnp.float32)
    derivative = normal_cdf + preact * normal_pdf
    delta = (residual * derivative).astype(jnp.bfloat16)
    product = lax.dot_general(
        batch_in, delta, (((0,), (0,)), ((), ())), preferred_element_type=jnp.float32
    )
    return product * fan_scale


def first_kernel(order, plan, x, t, *refs):
    weights, (mix, *shards), outs = refs[:HALVES], refs[HALVES:HALVES + 2 * STEPS - 1], refs[HALVES + 2 * STEPS - 1:]
    batch = x.shape[0] // STEPS
    rows = [pl.ds(pl.multiple_of(order[0, step] * batch, batch), batch) for step in range(STEPS)]
    mix[...] = jnp.zeros_like(mix)
    for step in range(STEPS):
        own, peer = [jnp.full((1, mix.shape[1]), plan[i, step].astype(jnp.float32)) for i in range(2)]
        mix[2 * step:2 * step + 1, :] = own / (own + peer)
        mix[2 * step + 1:2 * step + 2, :] = peer / (own + peer)
    own, _ = shares(mix, 0)
    width = weights[0].shape[1]
    for half, w in enumerate(weights):
        base, velocity = outs[2 * half:2 * half + 2]
        columns = slice(half * width, (half + 1) * width)
        gradient = gradient_of(x[rows[0], :], t[rows[0], columns], w[...])
        velocity[...] = gradient
        base[...] = own * w[...].astype(jnp.float32) - learning_rate * gradient
    for step in range(1, STEPS):
        shards[2 * step - 2][...] = x[rows[step], :]
        shards[2 * step - 1][...] = t[rows[step], :]


def middle_kernel(columns, mix, x, t, rounded, master, velocity_in, base, velocity):
    own, _ = shares(mix, 1)
    v = momentum_decay * velocity_in[...] + gradient_of(x[...], t[:, columns], rounded[...])
    velocity[...] = v
    base[...] = own * master[...] - learning_rate * v


def last_kernel(columns, split, mix, x, t, rounded, master, velocity_in, base, *outs):
    own, last_peer = shares(mix, STEPS - 1)
    r = rounded[...]
    v = momentum_decay * velocity_in[...] + gradient_of(x[...], t[:, columns], r)
    b = own * master[...] - learning_rate * v
    base[...] = b
    part = b + last_peer * r.astype(jnp.float32)
    if not split:
        outs[0][...] = part
        return
    keep, give, held = outs
    held[...] = part.reshape(held.shape)
    mine = lax.axis_index("gossip") & 1
    keep[...] = held[:, pl.ds(mine, 1)].reshape(keep.shape)
    give[...] = held[:, pl.ds(1 - mine, 1)].reshape(give.shape)


def round_kernel(step, mix, base, arrived, rounded, master):
    _, peer = shares(mix, step)
    total = base[...] + peer * arrived[...].astype(jnp.float32)
    rounded[...] = total.astype(jnp.bfloat16)
    master[...] = total


def finish_kernel(mix, base, arrived, *refs):
    _, peer = shares(mix, STEPS - 1)
    refs[-1][...] = (base[...] + peer * arrived[...].astype(jnp.float32)).astype(jnp.bfloat16)


def leg_kernel(axis, bit, kept, arrived, keep, give):
    mine = (lax.axis_index(axis) >> bit) & 1
    for out, side in ((keep, mine), (give, 1 - mine)):
        at = pl.ds(side, 1)
        total = kept[:, at] + arrived[:, at].astype(jnp.float32)
        out[...] = total.reshape(out.shape).astype(out.dtype)


def corner_kernel(first, first_arrived, second, second_arrived, keep, give_y, give_x, give_xy):
    y, x = (lax.axis_index("gossip") >> 1) & 1, lax.axis_index("group") & 1
    width = first.shape[-1]
    for out, row in ((keep, y), (give_y, 1 - y)):
        at, column = pl.ds(row, 1), pl.ds(x, 1)
        total = first[:, at] + first_arrived[:, at].astype(jnp.float32)
        out[:, :, :width] = total.reshape(out.shape[:-1] + (width,)).astype(out.dtype)
        total = second[:, at, column] + second_arrived[:, at, column]
        out[:, :, width:] = total.reshape(out.shape[:-1] + (width,)).astype(out.dtype)
    for out, row in ((give_x, y), (give_xy, 1 - y)):
        at, column = pl.ds(row, 1), pl.ds(1 - x, 1)
        total = second[:, at, column] + second_arrived[:, at, column]
        out[...] = total.reshape(out.shape).astype(out.dtype)


def spread_kernel(kept, from_y, from_x, from_xy, keep, *gives):
    mine = lax.axis_index("gossip") >> 2
    width = from_x.shape[-1]
    for other, out in enumerate((keep,) + gives):
        at = pl.ds(mine ^ other, 1)
        rows = kept[at] + from_y[at].astype(jnp.float32)
        late = from_x[at].astype(jnp.float32) + from_xy[at].astype(jnp.float32)
        out[:, :width] = rows[:, :, :width].reshape(out.shape[0], width).astype(out.dtype)
        out[:, width:] = (rows[:, :, width:] + late).reshape(out.shape[0], width).astype(out.dtype)


def final_kernel(replicas, mix, base, arrived, other_half, keep, *refs):
    out, mean = refs[-2:]
    finish_kernel(mix, base, arrived, other_half, out)
    total = keep[...]
    for piece in refs[:-2]:
        total = total + piece[...].astype(jnp.float32)
    mean[...] = total / replicas


IN_VMEM = pl.BlockSpec(memory_space=pltpu.VMEM)
IN_SMEM = pl.BlockSpec(memory_space=pltpu.SMEM)


def call(kernel, ins, outs, scratch=(), out_specs=None, in_place=None):
    in_specs = [IN_SMEM if array.dtype == jnp.int32 else IN_VMEM for array in ins]
    aliases = {}
    if in_place is not None:
        in_specs[in_place] = pl.BlockSpec(memory_space=pl.ANY)
        aliases = {in_place: 0}
    return pl.pallas_call(
        kernel,
        grid=(1,) if out_specs else (),
        in_specs=in_specs,
        out_specs=out_specs or [IN_VMEM] * len(outs),
        out_shape=[jax.ShapeDtypeStruct(shape, dtype) for shape, dtype in outs],
        scratch_shapes=list(scratch),
        input_output_aliases=aliases,
        compiler_params=pltpu.CompilerParams(vmem_limit_bytes=KERNEL_VMEM),
    )(*ins)


def scattered_sum(value):
    n_gossip, n_group = lax.axis_size("gossip"), lax.axis_size("group")
    gossip_bits, group_bits = n_gossip.bit_length() - 1, n_group.bit_length() - 1
    rows = value.shape[0]
    value = value.reshape((2,) * (gossip_bits + group_bits) + (rows // (n_gossip * n_group), value.shape[1]))
    left = [("gossip", bit) for bit in reversed(range(gossip_bits))]
    left += [("group", bit) for bit in reversed(range(group_bits))]
    order = [("gossip", 0)] + [("group", bit) for bit in range(group_bits)]
    order += [("gossip", bit) for bit in range(1, gossip_bits)]
    for axis, bit in order:
        place = left.index((axis, bit))
        mine = (lax.axis_index(axis) >> bit) & 1
        keep = lax.dynamic_index_in_dim(value, mine, place, keepdims=False)
        give = lax.dynamic_index_in_dim(value, 1 - mine, place, keepdims=False)
        value = keep + flipped(give, axis, 1 << bit)
        left.pop(place)
    return value


def steps(weights, inputs, targets, plan, order):
    n_gossip, n_group = lax.axis_size("gossip"), lax.axis_size("group")
    replicas = n_gossip * n_group
    weights = weights[0]
    din, dout = weights.shape
    width = dout // HALVES
    own_rows = din // replicas
    split = own_rows % 16 == 0 and n_group == 2 and n_gossip % 4 == 0
    columns = [slice(half * width, (half + 1) * width) for half in range(HALVES)]
    half_f32, half_bf16 = ((din, width), jnp.float32), ((din, width), jnp.bfloat16)

    plan = plan.T
    pieces, arrived0, rounds0, arrived1, middles = [], [], [], [], []
    for half in range(HALVES):
        pieces.append(weights[:, columns[half]])
        weights = lax.optimization_barrier(weights)
        arrived0.append(shifted(pieces[half], "gossip", 1))
    batch = inputs.shape[0] // STEPS
    shards = [((batch, din), inputs.dtype), ((batch, dout), targets.dtype)] * (STEPS - 1)
    outs = [((-(-2 * STEPS // 8) * 8, 128), jnp.float32)] + shards + [half_f32] * (2 * HALVES)
    mix, *rest = call(first_kernel, [order, plan, inputs, targets] + pieces, outs)
    shards, firsts = rest[:len(shards)], rest[len(shards):]
    for half in range(HALVES):
        rounds0.append(
            call(
                functools.partial(round_kernel, 0), [mix, firsts[2 * half], arrived0[half]], [half_bf16, half_f32]
            )
        )
        arrived1.append(shifted(rounds0[half][0], "gossip", 2))
    for half in range(HALVES):
        middles.append(
            call(
                functools.partial(middle_kernel, columns[half]),
                [mix] + shards[:2] + list(rounds0[half]) + [firsts[2 * half + 1]],
                [half_f32] * 2,
            )
        )
    parts, last = [], []
    for half in range(HALVES):
        base1, velocity1 = middles[half]
        rounded2, master2 = call(
            functools.partial(round_kernel, 1), [mix, base1, arrived1[half]], [half_bf16, half_f32]
        )
        arrived2 = shifted(rounded2, "gossip", 4)
        outs, scratch = [half_f32] * 2, ()
        if split:
            pair = (n_gossip // 2, n_group * own_rows, width)
            outs = [half_f32, (pair, jnp.float32), (pair, jnp.float32)]
            scratch = (pltpu.VMEM((pair[0], 2) + pair[1:], jnp.float32),)
        base2, *part = call(
            functools.partial(last_kernel, columns[half], split),
            [mix] + shards[2:] + [rounded2, master2, velocity1],
            outs,
            scratch,
        )
        last += [base2, arrived2]
        if not split:
            parts.append(part[0])
            continue
        keep, give = part
        got = flipped(give, "gossip", 1)
        if half < HALVES - 1:
            view = (n_gossip // 2, n_group, own_rows, width)
            shape = (n_gossip // 2, own_rows, width)
            keep, give = call(
                functools.partial(leg_kernel, "group", 0),
                [keep.reshape(view), got.reshape(view)],
                [(shape, jnp.float32), (shape, jnp.bfloat16)],
            )
            got = flipped(give, "group", 1)
        parts += [keep, got]
    if split:
        lead = n_gossip // 4
        view = (lead, 2, own_rows, width)
        deep = (lead, 2, n_group, own_rows, width)
        wide, narrow = (lead, own_rows, dout), (lead, own_rows, width)
        keep, give_y, give_x, give_xy = call(
            corner_kernel,
            [parts[0].reshape(view), parts[1].reshape(view), parts[2].reshape(deep), parts[3].reshape(deep)],
            [(wide, jnp.float32), (wide, jnp.bfloat16), (narrow, jnp.bfloat16), (narrow, jnp.bfloat16)],
        )
        from_x = flipped(give_x, "group", 1)
        from_y = flipped(give_y, "gossip", 2)
        pairs = [(source, source ^ (2 * n_group + 1)) for source in range(replicas)]
        from_xy = lax.ppermute(give_xy, ("gossip", "group"), pairs)
        shape = (own_rows, dout)
        others = [(shape, jnp.bfloat16)] * (lead - 1)
        keep, *gives = call(spread_kernel, [keep, from_y, from_x, from_xy], [(shape, jnp.float32)] + others)
        gots = []
        for other, give in enumerate(gives, 1):
            gots.append(flipped(give, "gossip", 4 * other))
    else:
        mean_weights = scattered_sum(jnp.concatenate(parts, axis=1)) / replicas
    result, replica_weights = ((din, dout), jnp.bfloat16), []
    for half in range(HALVES):
        ins = [mix, *last[2 * half:2 * half + 2], *replica_weights]
        block = pl.BlockSpec((din, width), lambda i, half=half: (0, half))
        in_place = 3 if half else None
        if split and half == HALVES - 1:
            *replica_weights, mean_weights = call(
                functools.partial(final_kernel, replicas), ins + [keep] + gots, [result, (shape, jnp.float32)],
                out_specs=[block, IN_VMEM], in_place=in_place,
            )
        else:
            replica_weights = call(finish_kernel, ins, [result], out_specs=[block], in_place=in_place)
    return (replica_weights[0][None], mean_weights)


def solution(mesh):
    return jax.shard_map(
        steps,
        mesh=mesh,
        in_specs=(
            P(("gossip", "group"), None, None),
            P(("gossip", "group"), None),
            P(("gossip", "group"), None),
            P(),
            P(("gossip", "group"), None),
        ),
        out_specs=(P(("gossip", "group"), None, None), P(("gossip", "group"), None)),
        check_vma=False,
    )
```

```python
import functools
import math

import jax
import jax.numpy as jnp
from jax import lax
from jax.experimental import pallas as pl
from jax.experimental.pallas import tpu as pltpu
from jax.sharding import PartitionSpec as P


STEPS = 3
HALVES = 2
KERNEL_VMEM = 20 << 20

learning_rate = 0.3
momentum_decay = 0.9


def shifted(value, axis, steps):
    count = lax.axis_size(axis)
    pairs = [(source, (source + steps) % count) for source in range(count)]
    return lax.ppermute(value, axis, pairs)


def moved(value, target):
    count = lax.axis_size("gossip")
    pairs = [(source, target(source) % count) for source in range(count) if target(source) is not None]
    return lax.ppermute(value, "gossip", pairs)


def flipped(value, axis, bit):
    count = lax.axis_size(axis)
    return lax.ppermute(value, axis, [(source, source ^ bit) for source in range(count)])


def shares(mix, step):
    return mix[2 * step:2 * step + 1, 0:1], mix[2 * step + 1:2 * step + 2, 0:1]


def gradient_of(batch_in, batch_out, rounded):
    fan_scale = 1.0 / math.sqrt(batch_in.shape[1])
    preact = jnp.dot(batch_in, rounded, preferred_element_type=jnp.float32) * fan_scale
    normal_cdf = 0.5 * (1.0 + lax.erf(preact * (1.0 / math.sqrt(2.0))))
    normal_pdf = jnp.exp(-0.5 * preact * preact) * (1.0 / math.sqrt(2.0 * math.pi))
    residual = preact * normal_cdf - batch_out.astype(jnp.float32)
    derivative = normal_cdf + preact * normal_pdf
    delta = (residual * derivative).astype(jnp.bfloat16)
    product = lax.dot_general(
        batch_in, delta, (((0,), (0,)), ((), ())), preferred_element_type=jnp.float32
    )
    return product * fan_scale


def piece_kernel(half, weights, piece, arrival):
    core, width = lax.axis_index("gossip") & 1, piece.shape[1]

    @pl.when(core == 1)
    def _():
        copy = pltpu.make_async_copy(weights.at[:, half * width:(half + 1) * width], piece, arrival)
        copy.start()
        copy.wait()

    @pl.when(core == 0)
    def _():
        piece[...] = jnp.zeros_like(piece)


def first_kernel(order, plan, x, t, *refs):
    weights, (mix, *shards), outs = refs[0], refs[1:2 * STEPS], refs[2 * STEPS:]
    batch = x.shape[0] // STEPS
    rows = [pl.ds(pl.multiple_of(order[0, step] * batch, batch), batch) for step in range(STEPS)]
    mix[...] = jnp.zeros_like(mix)
    for step in range(STEPS):
        own, peer = [jnp.full((1, mix.shape[1]), plan[i, step].astype(jnp.float32)) for i in range(2)]
        mix[2 * step:2 * step + 1, :] = own / (own + peer)
        mix[2 * step + 1:2 * step + 2, :] = peer / (own + peer)
    own, _ = shares(mix, 0)
    width = weights.shape[1] // HALVES
    for half in range(HALVES):
        base, velocity = outs[2 * half:2 * half + 2]
        columns = slice(half * width, (half + 1) * width)
        w = weights[:, columns]
        gradient = gradient_of(x[rows[0], :], t[rows[0], columns], w)
        velocity[...] = gradient
        base[...] = own * w.astype(jnp.float32) - learning_rate * gradient
    for step in range(1, STEPS):
        shards[2 * step - 2][...] = x[rows[step], :]
        shards[2 * step - 1][...] = t[rows[step], :]


def middle_kernel(columns, mix, x, t, rounded, master, velocity_in, base, velocity):
    own, _ = shares(mix, 1)
    v = momentum_decay * velocity_in[...] + gradient_of(x[...], t[:, columns], rounded[...])
    velocity[...] = v
    base[...] = own * master[...] - learning_rate * v


def last_kernel(columns, split, mix, x, t, rounded, master, velocity_in, base, *outs):
    own, last_peer = shares(mix, STEPS - 1)
    r = rounded[...]
    v = momentum_decay * velocity_in[...] + gradient_of(x[...], t[:, columns], r)
    b = own * master[...] - learning_rate * v
    base[...] = b
    part = b + last_peer * r.astype(jnp.float32)
    if not split:
        outs[0][...] = part
        return
    keep, give, held = outs
    held[...] = part.reshape(held.shape)
    mine = lax.axis_index("gossip") & 1
    keep[...] = held[:, pl.ds(mine, 1)].reshape(keep.shape)
    give[...] = held[:, pl.ds(1 - mine, 1)].reshape(give.shape)


def first_round_kernel(columns, mix, base, from_chip, on_chip, rounded, master):
    core = lax.axis_index("gossip") & 1
    pl.when(core == 0)(lambda: round_kernel(0, mix, base, from_chip, rounded, master))
    pl.when(core == 1)(lambda: round_kernel(0, mix, base, on_chip.at[:, columns], rounded, master))


def round_kernel(step, mix, base, arrived, rounded, master, *row_parts):
    _, peer = shares(mix, step)
    total = base[...] + peer * arrived[...].astype(jnp.float32)
    rounded[...] = total.astype(jnp.bfloat16)
    master[...] = total
    row = 0
    for part in row_parts:
        part[...] = rounded[row:row + part.shape[0], :]
        row += part.shape[0]


def finish_kernel(row, mix, base, arrived, *refs):
    _, peer = shares(mix, STEPS - 1)
    rows = slice(row, row + arrived.shape[0])
    refs[-1][...] = (base[rows, :] + peer * arrived[...].astype(jnp.float32)).astype(jnp.bfloat16)


def leg_kernel(axis, bit, kept, arrived, keep, give):
    mine = (lax.axis_index(axis) >> bit) & 1
    for out, side in ((keep, mine), (give, 1 - mine)):
        at = pl.ds(side, 1)
        total = kept[:, at] + arrived[:, at].astype(jnp.float32)
        out[...] = total.reshape(out.shape).astype(out.dtype)


def corner_kernel(first, first_arrived, second, second_arrived, keep, give_y, give_x, give_xy):
    y, x = (lax.axis_index("gossip") >> 1) & 1, lax.axis_index("group") & 1
    width = first.shape[-1]
    for out, row in ((keep, y), (give_y, 1 - y)):
        at, column = pl.ds(row, 1), pl.ds(x, 1)
        total = first[:, at] + first_arrived[:, at].astype(jnp.float32)
        out[:, :, :width] = total.reshape(out.shape[:-1] + (width,)).astype(out.dtype)
        total = second[:, at, column] + second_arrived[:, at, column]
        out[:, :, width:] = total.reshape(out.shape[:-1] + (width,)).astype(out.dtype)
    for out, row in ((give_x, y), (give_xy, 1 - y)):
        at, column = pl.ds(row, 1), pl.ds(1 - x, 1)
        total = second[:, at, column] + second_arrived[:, at, column]
        out[...] = total.reshape(out.shape).astype(out.dtype)


def spread_kernel(kept, from_y, from_x, from_xy, keep, *gives):
    mine = lax.axis_index("gossip") >> 2
    width = from_x.shape[-1]
    for other, out in enumerate((keep,) + gives):
        at = pl.ds(mine ^ other, 1)
        rows = kept[at] + from_y[at].astype(jnp.float32)
        late = from_x[at].astype(jnp.float32) + from_xy[at].astype(jnp.float32)
        out[:, :width] = rows[:, :, :width].reshape(out.shape[0], width).astype(out.dtype)
        out[:, width:] = (rows[:, :, width:] + late).reshape(out.shape[0], width).astype(out.dtype)


def mean_kernel(replicas, keep, *refs):
    total = keep[...]
    for piece in refs[:-1]:
        total = total + piece[...].astype(jnp.float32)
    refs[-1][...] = total / replicas


IN_VMEM = pl.BlockSpec(memory_space=pltpu.VMEM)
IN_SMEM = pl.BlockSpec(memory_space=pltpu.SMEM)


def call(kernel, ins, outs, scratch=(), out_specs=None, in_place=None, in_specs=None):
    in_specs = in_specs or [IN_SMEM if array.dtype == jnp.int32 else IN_VMEM for array in ins]
    aliases = {}
    if in_place is not None:
        in_specs[in_place] = pl.BlockSpec(memory_space=pl.ANY)
        aliases = {in_place: 0}
    return pl.pallas_call(
        kernel,
        grid=(1,) if out_specs else (),
        in_specs=in_specs,
        out_specs=out_specs or [IN_VMEM] * len(outs),
        out_shape=[jax.ShapeDtypeStruct(shape, dtype) for shape, dtype in outs],
        scratch_shapes=list(scratch),
        input_output_aliases=aliases,
        compiler_params=pltpu.CompilerParams(vmem_limit_bytes=KERNEL_VMEM),
    )(*ins)


def scattered_sum(value):
    n_gossip, n_group = lax.axis_size("gossip"), lax.axis_size("group")
    gossip_bits, group_bits = n_gossip.bit_length() - 1, n_group.bit_length() - 1
    rows = value.shape[0]
    value = value.reshape((2,) * (gossip_bits + group_bits) + (rows // (n_gossip * n_group), value.shape[1]))
    left = [("gossip", bit) for bit in reversed(range(gossip_bits))]
    left += [("group", bit) for bit in reversed(range(group_bits))]
    order = [("gossip", 0)] + [("group", bit) for bit in range(group_bits)]
    order += [("gossip", bit) for bit in range(1, gossip_bits)]
    for axis, bit in order:
        place = left.index((axis, bit))
        mine = (lax.axis_index(axis) >> bit) & 1
        keep = lax.dynamic_index_in_dim(value, mine, place, keepdims=False)
        give = lax.dynamic_index_in_dim(value, 1 - mine, place, keepdims=False)
        value = keep + flipped(give, axis, 1 << bit)
        left.pop(place)
    return value


def steps(weights, inputs, targets, plan, order):
    n_gossip, n_group = lax.axis_size("gossip"), lax.axis_size("group")
    replicas = n_gossip * n_group
    weights = weights[0]
    din, dout = weights.shape
    width = dout // HALVES
    own_rows = din // replicas
    split = own_rows % 16 == 0 and n_group == 2 and n_gossip % 4 == 0
    columns = [slice(half * width, (half + 1) * width) for half in range(HALVES)]
    half_f32, half_bf16 = ((din, width), jnp.float32), ((din, width), jnp.bfloat16)

    plan = plan.T
    in_hbm = pltpu.with_memory_space_constraint(weights, pltpu.HBM)
    pieces, arrived0, rounds0, arrived1, middles = [], [], [], [], []
    for half in range(HALVES):
        (piece,) = call(
            functools.partial(piece_kernel, half), [in_hbm], [half_bf16], (pltpu.SemaphoreType.DMA,),
            in_specs=[pl.BlockSpec(memory_space=pltpu.HBM)],
        )
        pieces.append(piece)
        arrived0.append(shifted(pieces[half], "gossip", 1))
    on_chip = moved(weights, lambda at: None if at & 1 else at + 1)
    batch = inputs.shape[0] // STEPS
    shards = [((batch, din), inputs.dtype), ((batch, dout), targets.dtype)] * (STEPS - 1)
    outs = [((-(-2 * STEPS // 8) * 8, 128), jnp.float32)] + shards + [half_f32] * (2 * HALVES)
    mix, *rest = call(first_kernel, [order, plan, inputs, targets, weights], outs)
    shards, firsts = rest[:len(shards)], rest[len(shards):]
    for half in range(HALVES):
        rounds0.append(
            call(
                functools.partial(first_round_kernel, columns[half]),
                [mix, firsts[2 * half], arrived0[half], on_chip],
                [half_bf16, half_f32],
            )
        )
        arrived1.append(shifted(rounds0[half][0], "gossip", 2))
    for half in range(HALVES):
        middles.append(
            call(
                functools.partial(middle_kernel, columns[half]),
                [mix] + shards[:2] + list(rounds0[half]) + [firsts[2 * half + 1]],
                [half_f32] * 2,
            )
        )
    parts, last = [], []
    for half in range(HALVES):
        base1, velocity1 = middles[half]
        heights = [din] if half < HALVES - 1 else [din - din // 4, din // 4]
        row_parts = [((height, width), jnp.bfloat16) for height in heights]
        rounded2, master2, *sent = call(
            functools.partial(round_kernel, 1), [mix, base1, arrived1[half]],
            [half_bf16, half_f32] + (row_parts if len(heights) > 1 else []),
        )
        arrived2 = shifted((sent or [rounded2])[0], "gossip", 4)
        outs, scratch = [half_f32] * 2, ()
        if split:
            pair = (n_gossip // 2, n_group * own_rows, width)
            outs = [half_f32, (pair, jnp.float32), (pair, jnp.float32)]
            scratch = (pltpu.VMEM((pair[0], 2) + pair[1:], jnp.float32),)
        base2, *part = call(
            functools.partial(last_kernel, columns[half], split),
            [mix] + shards[2:] + [rounded2, master2, velocity1],
            outs,
            scratch,
        )
        last.append((base2, arrived2))
        if not split:
            parts.append(part[0])
            continue
        keep, give = part
        got = flipped(give, "gossip", 1)
        if half < HALVES - 1:
            view = (n_gossip // 2, n_group, own_rows, width)
            shape = (n_gossip // 2, own_rows, width)
            keep, give = call(
                functools.partial(leg_kernel, "group", 0),
                [keep.reshape(view), got.reshape(view)],
                [(shape, jnp.float32), (shape, jnp.bfloat16)],
            )
            got = flipped(give, "group", 1)
        parts += [keep, got]
    if split:
        lead = n_gossip // 4
        view = (lead, 2, own_rows, width)
        deep = (lead, 2, n_group, own_rows, width)
        wide, narrow = (lead, own_rows, dout), (lead, own_rows, width)
        keep, give_y, give_x, give_xy = call(
            corner_kernel,
            [parts[0].reshape(view), parts[1].reshape(view), parts[2].reshape(deep), parts[3].reshape(deep)],
            [(wide, jnp.float32), (wide, jnp.bfloat16), (narrow, jnp.bfloat16), (narrow, jnp.bfloat16)],
        )
        from_x = flipped(give_x, "group", 1)
        from_y = flipped(give_y, "gossip", 2)
        pairs = [(source, source ^ (2 * n_group + 1)) for source in range(replicas)]
        from_xy = lax.ppermute(give_xy, ("gossip", "group"), pairs)
        shape = (own_rows, dout)
        others = [(shape, jnp.bfloat16)] * (lead - 1)
        keep, *gives = call(spread_kernel, [keep, from_y, from_x, from_xy], [(shape, jnp.float32)] + others)
        gots = []
        for other, give in enumerate(gives, 1):
            gots.append(flipped(give, "gossip", 4 * other))
    else:
        mean_weights = scattered_sum(jnp.concatenate(parts, axis=1)) / replicas
    arrived_tail = shifted(sent[1], "gossip", 4)
    result, replica_weights = ((din, dout), jnp.bfloat16), []
    for part in range(HALVES + 1):
        half = min(part, HALVES - 1)
        base2, arrived2 = last[half]
        row = din - din // 4 if part == HALVES else 0
        arrived2 = arrived_tail if row else arrived2
        height = arrived2.shape[0]
        block = pl.BlockSpec((height, width), lambda i, at=(row // height, half): at)
        replica_weights = call(
            functools.partial(finish_kernel, row), [mix, base2, arrived2, *replica_weights], [result],
            out_specs=[block], in_place=3 if part else None,
        )
    if split:
        (mean_weights,) = call(functools.partial(mean_kernel, replicas), [keep] + gots, [(shape, jnp.float32)])
    return (replica_weights[0][None], mean_weights)


def solution(mesh):
    return jax.shard_map(
        steps,
        mesh=mesh,
        in_specs=(
            P(("gossip", "group"), None, None),
            P(("gossip", "group"), None),
            P(("gossip", "group"), None),
            P(),
            P(("gossip", "group"), None),
        ),
        out_specs=(P(("gossip", "group"), None, None), P(("gossip", "group"), None)),
        check_vma=False,
    )
```

```python
import functools
import math

import jax
import jax.numpy as jnp
from jax import lax
from jax.experimental import pallas as pl
from jax.experimental.pallas import tpu as pltpu
from jax.sharding import PartitionSpec as P


STEPS = 3
HALVES = 2
KERNEL_VMEM = 20 << 20

learning_rate = 0.3
momentum_decay = 0.9


def shifted(value, axis, steps):
    count = lax.axis_size(axis)
    pairs = [(source, (source + steps) % count) for source in range(count)]
    return lax.ppermute(value, axis, pairs)


def moved(value, target):
    count = lax.axis_size("gossip")
    pairs = [(source, target(source) % count) for source in range(count) if target(source) is not None]
    return lax.ppermute(value, "gossip", pairs)


def flipped(value, axis, bit):
    count = lax.axis_size(axis)
    return lax.ppermute(value, axis, [(source, source ^ bit) for source in range(count)])


def shares(mix, step):
    return mix[2 * step:2 * step + 1, 0:1], mix[2 * step + 1:2 * step + 2, 0:1]


def gradient_of(batch_in, batch_out, rounded):
    fan_scale = 1.0 / math.sqrt(batch_in.shape[1])
    preact = jnp.dot(batch_in, rounded, preferred_element_type=jnp.float32) * fan_scale
    normal_cdf = 0.5 * (1.0 + lax.erf(preact * (1.0 / math.sqrt(2.0))))
    normal_pdf = jnp.exp(-0.5 * preact * preact) * (1.0 / math.sqrt(2.0 * math.pi))
    residual = preact * normal_cdf - batch_out.astype(jnp.float32)
    derivative = normal_cdf + preact * normal_pdf
    delta = (residual * derivative).astype(jnp.bfloat16)
    product = lax.dot_general(
        batch_in, delta, (((0,), (0,)), ((), ())), preferred_element_type=jnp.float32
    )
    return product * fan_scale


def piece_kernel(half, weights, piece, arrival):
    core, width = lax.axis_index("gossip") & 1, piece.shape[1]

    @pl.when(core == 1)
    def _():
        copy = pltpu.make_async_copy(weights.at[:, half * width:(half + 1) * width], piece, arrival)
        copy.start()
        copy.wait()

    @pl.when(core == 0)
    def _():
        piece[...] = jnp.zeros_like(piece)


def first_kernel(order, plan, x, t, *refs):
    weights, (mix, *shards), outs = refs[0], refs[1:2 * STEPS], refs[2 * STEPS:]
    batch = x.shape[0] // STEPS
    rows = [pl.ds(pl.multiple_of(order[0, step] * batch, batch), batch) for step in range(STEPS)]
    mix[...] = jnp.zeros_like(mix)
    for step in range(STEPS):
        own, peer = [jnp.full((1, mix.shape[1]), plan[i, step].astype(jnp.float32)) for i in range(2)]
        mix[2 * step:2 * step + 1, :] = own / (own + peer)
        mix[2 * step + 1:2 * step + 2, :] = peer / (own + peer)
    own, _ = shares(mix, 0)
    width = weights.shape[1] // HALVES
    for half in range(HALVES):
        base, velocity = outs[2 * half:2 * half + 2]
        columns = slice(half * width, (half + 1) * width)
        w = weights[:, columns]
        gradient = gradient_of(x[rows[0], :], t[rows[0], columns], w)
        velocity[...] = gradient
        base[...] = own * w.astype(jnp.float32) - learning_rate * gradient
    for step in range(1, STEPS):
        shards[2 * step - 2][...] = x[rows[step], :]
        shards[2 * step - 1][...] = t[rows[step], :]


def middle_kernel(columns, mix, x, t, rounded, master, velocity_in, base, velocity):
    own, _ = shares(mix, 1)
    v = momentum_decay * velocity_in[...] + gradient_of(x[...], t[:, columns], rounded[...])
    velocity[...] = v
    base[...] = own * master[...] - learning_rate * v


def last_kernel(columns, split, mix, x, t, rounded, master, velocity_in, base, *outs):
    own, last_peer = shares(mix, STEPS - 1)
    r = rounded[...]
    v = momentum_decay * velocity_in[...] + gradient_of(x[...], t[:, columns], r)
    b = own * master[...] - learning_rate * v
    base[...] = b
    part = b + last_peer * r.astype(jnp.float32)
    if not split:
        outs[0][...] = part
        return
    keep, give, held = outs
    held[...] = part.reshape(held.shape)
    mine = lax.axis_index("gossip") & 1
    keep[...] = held[:, pl.ds(mine, 1)].reshape(keep.shape)
    give[...] = held[:, pl.ds(1 - mine, 1)].reshape(give.shape)


def first_round_kernel(columns, mix, base, from_chip, on_chip, rounded, master):
    core = lax.axis_index("gossip") & 1
    pl.when(core == 0)(lambda: round_kernel(0, mix, base, from_chip, rounded, master))
    pl.when(core == 1)(lambda: round_kernel(0, mix, base, on_chip.at[:, columns], rounded, master))


def round_kernel(step, mix, base, arrived, rounded, master):
    _, peer = shares(mix, step)
    total = base[...] + peer * arrived[...].astype(jnp.float32)
    rounded[...] = total.astype(jnp.bfloat16)
    master[...] = total


def finish_kernel(mix, base, arrived, *refs):
    _, peer = shares(mix, STEPS - 1)
    refs[-1][...] = (base[...] + peer * arrived[...].astype(jnp.float32)).astype(jnp.bfloat16)


def leg_kernel(axis, bit, kept, arrived, keep, give):
    mine = (lax.axis_index(axis) >> bit) & 1
    for out, side in ((keep, mine), (give, 1 - mine)):
        at = pl.ds(side, 1)
        total = kept[:, at] + arrived[:, at].astype(jnp.float32)
        out[...] = total.reshape(out.shape).astype(out.dtype)


def corner_kernel(first, first_arrived, second, second_arrived, keep, give_y, give_x, give_xy):
    at = lax.axis_index("gossip")
    own, y, x = at >> 2, (at >> 1) & 1, lax.axis_index("group") & 1
    width, half = first.shape[-1], first.shape[0] // 2
    for near, wide, narrow in ((y, keep, give_x), (1 - y, give_y, give_xy)):
        for i in range(half):
            block = pl.ds(own ^ ((1 - near) * half + i), 1)
            for row in range(2):
                to = (slice(2 * i + row, 2 * i + row + 1), slice(None))
                shape = (1, wide.shape[1], width)
                total = first[block, row] + first_arrived[block, row].astype(jnp.float32)
                wide[to + (slice(0, width),)] = total.reshape(shape).astype(wide.dtype)
                for out, side, columns in ((wide, x, slice(width, None)), (narrow, 1 - x, slice(None))):
                    column = pl.ds(side, 1)
                    total = second[block, row, column] + second_arrived[block, row, column]
                    out[to + (columns,)] = total.reshape(shape).astype(out.dtype)


def spread_kernel(kept, from_y, from_x, from_xy, keep, *gives):
    y = (lax.axis_index("gossip") >> 1) & 1
    width = from_x.shape[-1]

    def block_of(place, out):
        at = pl.ds(place, 1)
        rows = kept[at] + from_y[at].astype(jnp.float32)
        late = from_x[at].astype(jnp.float32) + from_xy[at].astype(jnp.float32)
        out[:, :width] = rows[:, :, :width].reshape(out.shape[0], width).astype(out.dtype)
        out[:, width:] = (rows[:, :, width:] + late).reshape(out.shape[0], width).astype(out.dtype)

    block_of(1, keep)
    keep[...] = jnp.where(y == 1, keep[...], 0.0)
    for i in range(len(gives) // 2):
        block_of(2 * i + y, gives[2 * i])
        block_of(2 * i + 1 - y, gives[2 * i + 1])


def mean_kernel(replicas, keep, *refs):
    total = keep[...]
    for piece in refs[:-1]:
        total = total + piece[...].astype(jnp.float32)
    refs[-1][...] = total / replicas


IN_VMEM = pl.BlockSpec(memory_space=pltpu.VMEM)
IN_SMEM = pl.BlockSpec(memory_space=pltpu.SMEM)


def call(kernel, ins, outs, scratch=(), out_specs=None, in_place=None, in_specs=None):
    in_specs = in_specs or [IN_SMEM if array.dtype == jnp.int32 else IN_VMEM for array in ins]
    aliases = {}
    if in_place is not None:
        in_specs[in_place] = pl.BlockSpec(memory_space=pl.ANY)
        aliases = {in_place: 0}
    return pl.pallas_call(
        kernel,
        grid=(1,) if out_specs else (),
        in_specs=in_specs,
        out_specs=out_specs or [IN_VMEM] * len(outs),
        out_shape=[jax.ShapeDtypeStruct(shape, dtype) for shape, dtype in outs],
        scratch_shapes=list(scratch),
        input_output_aliases=aliases,
        compiler_params=pltpu.CompilerParams(vmem_limit_bytes=KERNEL_VMEM),
    )(*ins)


def scattered_sum(value):
    n_gossip, n_group = lax.axis_size("gossip"), lax.axis_size("group")
    gossip_bits, group_bits = n_gossip.bit_length() - 1, n_group.bit_length() - 1
    rows = value.shape[0]
    value = value.reshape((2,) * (gossip_bits + group_bits) + (rows // (n_gossip * n_group), value.shape[1]))
    left = [("gossip", bit) for bit in reversed(range(gossip_bits))]
    left += [("group", bit) for bit in reversed(range(group_bits))]
    order = [("gossip", 0)] + [("group", bit) for bit in range(group_bits)]
    order += [("gossip", bit) for bit in range(1, gossip_bits)]
    for axis, bit in order:
        place = left.index((axis, bit))
        mine = (lax.axis_index(axis) >> bit) & 1
        keep = lax.dynamic_index_in_dim(value, mine, place, keepdims=False)
        give = lax.dynamic_index_in_dim(value, 1 - mine, place, keepdims=False)
        value = keep + flipped(give, axis, 1 << bit)
        left.pop(place)
    return value


def steps(weights, inputs, targets, plan, order):
    n_gossip, n_group = lax.axis_size("gossip"), lax.axis_size("group")
    replicas = n_gossip * n_group
    weights = weights[0]
    din, dout = weights.shape
    width = dout // HALVES
    own_rows = din // replicas
    split = own_rows % 16 == 0 and n_group == 2 and n_gossip % 4 == 0
    columns = [slice(half * width, (half + 1) * width) for half in range(HALVES)]
    half_f32, half_bf16 = ((din, width), jnp.float32), ((din, width), jnp.bfloat16)

    plan = plan.T
    in_hbm = pltpu.with_memory_space_constraint(weights, pltpu.HBM)
    pieces, arrived0, rounds0, arrived1, middles = [], [], [], [], []
    for half in range(HALVES):
        (piece,) = call(
            functools.partial(piece_kernel, half), [in_hbm], [half_bf16], (pltpu.SemaphoreType.DMA,),
            in_specs=[pl.BlockSpec(memory_space=pltpu.HBM)],
        )
        pieces.append(piece)
        arrived0.append(shifted(pieces[half], "gossip", 1))
    on_chip = moved(weights, lambda at: None if at & 1 else at + 1)
    batch = inputs.shape[0] // STEPS
    shards = [((batch, din), inputs.dtype), ((batch, dout), targets.dtype)] * (STEPS - 1)
    outs = [((-(-2 * STEPS // 8) * 8, 128), jnp.float32)] + shards + [half_f32] * (2 * HALVES)
    mix, *rest = call(first_kernel, [order, plan, inputs, targets, weights], outs)
    shards, firsts = rest[:len(shards)], rest[len(shards):]
    for half in range(HALVES):
        rounds0.append(
            call(
                functools.partial(first_round_kernel, columns[half]),
                [mix, firsts[2 * half], arrived0[half], on_chip],
                [half_bf16, half_f32],
            )
        )
        arrived1.append(shifted(rounds0[half][0], "gossip", 2))
    for half in range(HALVES):
        middles.append(
            call(
                functools.partial(middle_kernel, columns[half]),
                [mix] + shards[:2] + list(rounds0[half]) + [firsts[2 * half + 1]],
                [half_f32] * 2,
            )
        )
    parts, last = [], []
    for half in range(HALVES):
        base1, velocity1 = middles[half]
        rounded2, master2 = call(
            functools.partial(round_kernel, 1), [mix, base1, arrived1[half]], [half_bf16, half_f32]
        )
        arrived2 = shifted(rounded2, "gossip", 4)
        outs, scratch = [half_f32] * 2, ()
        if split:
            pair = (n_gossip // 2, n_group * own_rows, width)
            outs = [half_f32, (pair, jnp.float32), (pair, jnp.float32)]
            scratch = (pltpu.VMEM((pair[0], 2) + pair[1:], jnp.float32),)
        base2, *part = call(
            functools.partial(last_kernel, columns[half], split),
            [mix] + shards[2:] + [rounded2, master2, velocity1],
            outs,
            scratch,
        )
        last += [base2, arrived2]
        if not split:
            parts.append(part[0])
            continue
        keep, give = part
        got = flipped(give, "gossip", 1)
        if half < HALVES - 1:
            view = (n_gossip // 2, n_group, own_rows, width)
            shape = (n_gossip // 2, own_rows, width)
            keep, give = call(
                functools.partial(leg_kernel, "group", 0),
                [keep.reshape(view), got.reshape(view)],
                [(shape, jnp.float32), (shape, jnp.bfloat16)],
            )
            got = flipped(give, "group", 1)
        parts += [keep, got]
    if split:
        lead = n_gossip // 4
        view = (lead, 2, own_rows, width)
        deep = (lead, 2, n_group, own_rows, width)
        wide, narrow = (lead, own_rows, dout), (lead, own_rows, width)
        keep, give_y, give_x, give_xy = call(
            corner_kernel,
            [parts[0].reshape(view), parts[1].reshape(view), parts[2].reshape(deep), parts[3].reshape(deep)],
            [(wide, jnp.float32), (wide, jnp.bfloat16), (narrow, jnp.bfloat16), (narrow, jnp.bfloat16)],
        )
        from_x = flipped(give_x, "group", 1)
        from_y = flipped(give_y, "gossip", 2)
        pairs = [(source, source ^ (2 * n_group + 1)) for source in range(replicas)]
        from_xy = lax.ppermute(give_xy, ("gossip", "group"), pairs)
        shape = (own_rows, dout)
        others = [(shape, jnp.bfloat16)] * lead
        keep, *gives = call(spread_kernel, [keep, from_y, from_x, from_xy], [(shape, jnp.float32)] + others)
        gots = []
        for i in range(lead // 2):
            for cross in range(2):

                def target(at, i=i, cross=cross):
                    own, y, core = at >> 2, (at >> 1) & 1, at & 1
                    if y and not i and not cross:
                        return None
                    return ((own ^ (i if y else lead // 2 + i)) << 2) | ((y ^ cross) << 1) | core

                gots.append(moved(gives[2 * i + cross], target))
    else:
        mean_weights = scattered_sum(jnp.concatenate(parts, axis=1)) / replicas
    result, replica_weights = ((din, dout), jnp.bfloat16), []
    for half in range(HALVES):
        replica_weights = call(
            finish_kernel,
            [mix, *last[2 * half:2 * half + 2], *replica_weights],
            [result],
            out_specs=[pl.BlockSpec((din, width), lambda i, half=half: (0, half))],
            in_place=3 if half else None,
        )
    if split:
        (mean_weights,) = call(functools.partial(mean_kernel, replicas), [keep] + gots, [(shape, jnp.float32)])
    return (replica_weights[0][None], mean_weights)


def solution(mesh):
    return jax.shard_map(
        steps,
        mesh=mesh,
        in_specs=(
            P(("gossip", "group"), None, None),
            P(("gossip", "group"), None),
            P(("gossip", "group"), None),
            P(),
            P(("gossip", "group"), None),
        ),
        out_specs=(P(("gossip", "group"), None, None), P(("gossip", "group"), None)),
        check_vma=False,
    )
```

```python
import functools
import math

import jax
import jax.numpy as jnp
from jax import lax
from jax.experimental import pallas as pl
from jax.experimental.pallas import tpu as pltpu
from jax.sharding import PartitionSpec as P


STEPS = 3
HALVES = 2
KERNEL_VMEM = 20 << 20

learning_rate = 0.3
momentum_decay = 0.9


def shifted(value, axis, steps):
    count = lax.axis_size(axis)
    pairs = [(source, (source + steps) % count) for source in range(count)]
    return lax.ppermute(value, axis, pairs)


def moved(value, target):
    count = lax.axis_size("gossip")
    pairs = [(source, target(source) % count) for source in range(count) if target(source) is not None]
    return lax.ppermute(value, "gossip", pairs)


def flipped(value, axis, bit):
    count = lax.axis_size(axis)
    return lax.ppermute(value, axis, [(source, source ^ bit) for source in range(count)])


def shares(mix, step):
    return mix[2 * step:2 * step + 1, 0:1], mix[2 * step + 1:2 * step + 2, 0:1]


def gradient_of(batch_in, batch_out, rounded):
    fan_scale = 1.0 / math.sqrt(batch_in.shape[1])
    preact = jnp.dot(batch_in, rounded, preferred_element_type=jnp.float32) * fan_scale
    normal_cdf = 0.5 * (1.0 + lax.erf(preact * (1.0 / math.sqrt(2.0))))
    normal_pdf = jnp.exp(-0.5 * preact * preact) * (1.0 / math.sqrt(2.0 * math.pi))
    residual = preact * normal_cdf - batch_out.astype(jnp.float32)
    derivative = normal_cdf + preact * normal_pdf
    delta = (residual * derivative).astype(jnp.bfloat16)
    product = lax.dot_general(
        batch_in, delta, (((0,), (0,)), ((), ())), preferred_element_type=jnp.float32
    )
    return product * fan_scale


def piece_kernel(half, weights, piece, arrival):
    core, width = lax.axis_index("gossip") & 1, piece.shape[1]

    @pl.when(core == 1)
    def _():
        copy = pltpu.make_async_copy(weights.at[:, half * width:(half + 1) * width], piece, arrival)
        copy.start()
        copy.wait()

    @pl.when(core == 0)
    def _():
        piece[...] = jnp.zeros_like(piece)


def first_kernel(order, plan, x, t, *refs):
    weights, (mix, *shards), outs = refs[0], refs[1:2 * STEPS], refs[2 * STEPS:]
    batch = x.shape[0] // STEPS
    rows = [pl.ds(pl.multiple_of(order[0, step] * batch, batch), batch) for step in range(STEPS)]
    mix[...] = jnp.zeros_like(mix)
    for step in range(STEPS):
        own, peer = [jnp.full((1, mix.shape[1]), plan[i, step].astype(jnp.float32)) for i in range(2)]
        mix[2 * step:2 * step + 1, :] = own / (own + peer)
        mix[2 * step + 1:2 * step + 2, :] = peer / (own + peer)
    own, _ = shares(mix, 0)
    width = weights.shape[1] // HALVES
    for half in range(HALVES):
        base, velocity = outs[2 * half:2 * half + 2]
        columns = slice(half * width, (half + 1) * width)
        w = weights[:, columns]
        gradient = gradient_of(x[rows[0], :], t[rows[0], columns], w)
        velocity[...] = gradient
        base[...] = own * w.astype(jnp.float32) - learning_rate * gradient
    for step in range(1, STEPS):
        shards[2 * step - 2][...] = x[rows[step], :]
        shards[2 * step - 1][...] = t[rows[step], :]


def middle_kernel(columns, mix, x, t, rounded, master, velocity_in, base, velocity):
    own, _ = shares(mix, 1)
    v = momentum_decay * velocity_in[...] + gradient_of(x[...], t[:, columns], rounded[...])
    velocity[...] = v
    base[...] = own * master[...] - learning_rate * v


def last_kernel(columns, split, mix, x, t, rounded, master, velocity_in, base, *outs):
    own, last_peer = shares(mix, STEPS - 1)
    r = rounded[...]
    v = momentum_decay * velocity_in[...] + gradient_of(x[...], t[:, columns], r)
    b = own * master[...] - learning_rate * v
    base[...] = b
    part = b + last_peer * r.astype(jnp.float32)
    if not split:
        outs[0][...] = part
        return
    keep, give, held = outs
    held[...] = part.reshape(held.shape)
    mine = lax.axis_index("gossip") & 1
    keep[...] = held[:, pl.ds(mine, 1)].reshape(keep.shape)
    give[...] = held[:, pl.ds(1 - mine, 1)].reshape(give.shape)


def first_round_kernel(columns, mix, base, from_chip, on_chip, rounded, master):
    core = lax.axis_index("gossip") & 1
    pl.when(core == 0)(lambda: round_kernel(0, mix, base, from_chip, rounded, master))
    pl.when(core == 1)(lambda: round_kernel(0, mix, base, on_chip.at[:, columns], rounded, master))


def round_kernel(step, mix, base, arrived, rounded, master):
    _, peer = shares(mix, step)
    total = base[...] + peer * arrived[...].astype(jnp.float32)
    rounded[...] = total.astype(jnp.bfloat16)
    master[...] = total


def finish_kernel(mix, base, arrived, *refs):
    _, peer = shares(mix, STEPS - 1)
    refs[-1][...] = (base[...] + peer * arrived[...].astype(jnp.float32)).astype(jnp.bfloat16)


def leg_kernel(axis, bit, kept, arrived, keep, give):
    mine = (lax.axis_index(axis) >> bit) & 1
    for out, side in ((keep, mine), (give, 1 - mine)):
        at = pl.ds(side, 1)
        total = kept[:, at] + arrived[:, at].astype(jnp.float32)
        out[...] = total.reshape(out.shape).astype(out.dtype)


def corner_kernel(first, first_arrived, second, second_arrived, keep, give_y, give_x, give_xy):
    y, x = (lax.axis_index("gossip") >> 1) & 1, lax.axis_index("group") & 1
    width = first.shape[-1]
    for out, row in ((keep, y), (give_y, 1 - y)):
        at, column = pl.ds(row, 1), pl.ds(x, 1)
        total = first[:, at] + first_arrived[:, at].astype(jnp.float32)
        out[:, :, :width] = total.reshape(out.shape[:-1] + (width,)).astype(out.dtype)
        total = second[:, at, column] + second_arrived[:, at, column]
        out[:, :, width:] = total.reshape(out.shape[:-1] + (width,)).astype(out.dtype)
    for out, row in ((give_x, y), (give_xy, 1 - y)):
        at, column = pl.ds(row, 1), pl.ds(1 - x, 1)
        total = second[:, at, column] + second_arrived[:, at, column]
        out[...] = total.reshape(out.shape).astype(out.dtype)


def spread_kernel(kept, from_y, from_x, from_xy, keep, *gives):
    mine = lax.axis_index("gossip") >> 2
    width = from_x.shape[-1]
    for other, out in enumerate((keep,) + gives):
        at = pl.ds(mine ^ other, 1)
        rows = kept[at] + from_y[at].astype(jnp.float32)
        late = from_x[at].astype(jnp.float32) + from_xy[at].astype(jnp.float32)
        out[:, :width] = rows[:, :, :width].reshape(out.shape[0], width).astype(out.dtype)
        out[:, width:] = (rows[:, :, width:] + late).reshape(out.shape[0], width).astype(out.dtype)


def mean_kernel(replicas, keep, *refs):
    total = keep[...]
    for piece in refs[:-1]:
        total = total + piece[...].astype(jnp.float32)
    refs[-1][...] = total / replicas


IN_VMEM = pl.BlockSpec(memory_space=pltpu.VMEM)
IN_SMEM = pl.BlockSpec(memory_space=pltpu.SMEM)


def call(kernel, ins, outs, scratch=(), out_specs=None, in_place=None, in_specs=None):
    in_specs = in_specs or [IN_SMEM if array.dtype == jnp.int32 else IN_VMEM for array in ins]
    aliases = {}
    if in_place is not None:
        in_specs[in_place] = pl.BlockSpec(memory_space=pl.ANY)
        aliases = {in_place: 0}
    return pl.pallas_call(
        kernel,
        grid=(1,) if out_specs else (),
        in_specs=in_specs,
        out_specs=out_specs or [IN_VMEM] * len(outs),
        out_shape=[jax.ShapeDtypeStruct(shape, dtype) for shape, dtype in outs],
        scratch_shapes=list(scratch),
        input_output_aliases=aliases,
        compiler_params=pltpu.CompilerParams(vmem_limit_bytes=KERNEL_VMEM),
    )(*ins)


def scattered_sum(value):
    n_gossip, n_group = lax.axis_size("gossip"), lax.axis_size("group")
    gossip_bits, group_bits = n_gossip.bit_length() - 1, n_group.bit_length() - 1
    rows = value.shape[0]
    value = value.reshape((2,) * (gossip_bits + group_bits) + (rows // (n_gossip * n_group), value.shape[1]))
    left = [("gossip", bit) for bit in reversed(range(gossip_bits))]
    left += [("group", bit) for bit in reversed(range(group_bits))]
    order = [("gossip", 0)] + [("group", bit) for bit in range(group_bits)]
    order += [("gossip", bit) for bit in range(1, gossip_bits)]
    for axis, bit in order:
        place = left.index((axis, bit))
        mine = (lax.axis_index(axis) >> bit) & 1
        keep = lax.dynamic_index_in_dim(value, mine, place, keepdims=False)
        give = lax.dynamic_index_in_dim(value, 1 - mine, place, keepdims=False)
        value = keep + flipped(give, axis, 1 << bit)
        left.pop(place)
    return value


def steps(weights, inputs, targets, plan, order):
    n_gossip, n_group = lax.axis_size("gossip"), lax.axis_size("group")
    replicas = n_gossip * n_group
    weights = weights[0]
    din, dout = weights.shape
    width = dout // HALVES
    own_rows = din // replicas
    split = own_rows % 16 == 0 and n_group == 2 and n_gossip % 4 == 0
    columns = [slice(half * width, (half + 1) * width) for half in range(HALVES)]
    half_f32, half_bf16 = ((din, width), jnp.float32), ((din, width), jnp.bfloat16)

    plan = plan.T
    in_hbm = pltpu.with_memory_space_constraint(weights, pltpu.HBM)
    pieces, arrived0, rounds0, arrived1, middles = [], [], [], [], []
    for half in range(HALVES):
        (piece,) = call(
            functools.partial(piece_kernel, half), [in_hbm], [half_bf16], (pltpu.SemaphoreType.DMA,),
            in_specs=[pl.BlockSpec(memory_space=pltpu.HBM)],
        )
        pieces.append(piece)
        arrived0.append(shifted(pieces[half], "gossip", 1))
    on_chip = moved(weights, lambda at: None if at & 1 else at + 1)
    batch = inputs.shape[0] // STEPS
    shards = [((batch, din), inputs.dtype), ((batch, dout), targets.dtype)] * (STEPS - 1)
    outs = [((-(-2 * STEPS // 8) * 8, 128), jnp.float32)] + shards + [half_f32] * (2 * HALVES)
    mix, *rest = call(first_kernel, [order, plan, inputs, targets, weights], outs)
    shards, firsts = rest[:len(shards)], rest[len(shards):]
    for half in range(HALVES):
        rounds0.append(
            call(
                functools.partial(first_round_kernel, columns[half]),
                [mix, firsts[2 * half], arrived0[half], on_chip],
                [half_bf16, half_f32],
            )
        )
        arrived1.append(shifted(rounds0[half][0], "gossip", 2))
    for half in range(HALVES):
        middles.append(
            call(
                functools.partial(middle_kernel, columns[half]),
                [mix] + shards[:2] + list(rounds0[half]) + [firsts[2 * half + 1]],
                [half_f32] * 2,
            )
        )
    parts, last = [], []
    for half in range(HALVES):
        base1, velocity1 = middles[half]
        rounded2, master2 = call(
            functools.partial(round_kernel, 1), [mix, base1, arrived1[half]], [half_bf16, half_f32]
        )
        arrived2 = shifted(rounded2, "gossip", 4)
        outs, scratch = [half_f32] * 2, ()
        if split:
            pair = (n_gossip // 2, n_group * own_rows, width)
            outs = [half_f32, (pair, jnp.float32), (pair, jnp.float32)]
            scratch = (pltpu.VMEM((pair[0], 2) + pair[1:], jnp.float32),)
        base2, *part = call(
            functools.partial(last_kernel, columns[half], split),
            [mix] + shards[2:] + [rounded2, master2, velocity1],
            outs,
            scratch,
        )
        last += [base2, arrived2]
        if not split:
            parts.append(part[0])
            continue
        keep, give = part
        got = flipped(give, "gossip", 1)
        if half < HALVES - 1:
            view = (n_gossip // 2, n_group, own_rows, width)
            shape = (n_gossip // 2, own_rows, width)
            keep, give = call(
                functools.partial(leg_kernel, "group", 0),
                [keep.reshape(view), got.reshape(view)],
                [(shape, jnp.float32), (shape, jnp.bfloat16)],
            )
            got = flipped(give, "group", 1)
        parts += [keep, got]
    if split:
        lead = n_gossip // 4
        view = (lead, 2, own_rows, width)
        deep = (lead, 2, n_group, own_rows, width)
        wide, narrow = (lead, own_rows, dout), (lead, own_rows, width)
        keep, give_y, give_x, give_xy = call(
            corner_kernel,
            [parts[0].reshape(view), parts[1].reshape(view), parts[2].reshape(deep), parts[3].reshape(deep)],
            [(wide, jnp.float32), (wide, jnp.bfloat16), (narrow, jnp.bfloat16), (narrow, jnp.bfloat16)],
        )
        from_x = flipped(give_x, "group", 1)
        from_y = flipped(give_y, "gossip", 2)
        pairs = [(source, source ^ (2 * n_group + 1)) for source in range(replicas)]
        from_xy = lax.ppermute(give_xy, ("gossip", "group"), pairs)
        shape = (own_rows, dout)
        others = [(shape, jnp.bfloat16)] * (lead - 1)
        keep, *gives = call(spread_kernel, [keep, from_y, from_x, from_xy], [(shape, jnp.float32)] + others)
        gots = []
        for other, give in enumerate(gives, 1):
            gots.append(flipped(give, "gossip", 4 * other))
    else:
        mean_weights = scattered_sum(jnp.concatenate(parts, axis=1)) / replicas
    result, replica_weights = ((din, dout), jnp.bfloat16), []
    for half in range(HALVES):
        replica_weights = call(
            finish_kernel,
            [mix, *last[2 * half:2 * half + 2], *replica_weights],
            [result],
            out_specs=[pl.BlockSpec((din, width), lambda i, half=half: (0, half))],
            in_place=3 if half else None,
        )
    if split:
        (mean_weights,) = call(functools.partial(mean_kernel, replicas), [keep] + gots, [(shape, jnp.float32)])
    return (replica_weights[0][None], mean_weights)


def solution(mesh):
    return jax.shard_map(
        steps,
        mesh=mesh,
        in_specs=(
            P(("gossip", "group"), None, None),
            P(("gossip", "group"), None),
            P(("gossip", "group"), None),
            P(),
            P(("gossip", "group"), None),
        ),
        out_specs=(P(("gossip", "group"), None, None), P(("gossip", "group"), None)),
        check_vma=False,
    )
```
